256 devices in a mesh: sub: 32 (over z, x_hi, core), rng: 8 (over y, x_lo).
Axes of the slice: x: 4 (x_hi: 2, x_lo: 2; x = x_hi * 2 + x_lo), y: 4, z: 8, core: 2. Of those that a mesh axis runs over, the one named last changes fastest.
Arguments:
- raw_echoes: bfloat16 [2, 32768, 4096], P(None, ('sub', 'rng')), may hold values from -6 to 6
- merge_taps: int32 [4, 2, 8, 512], replicated, may hold values from 0 to 255
- merge_weights: float32 [4, 2, 8, 512], replicated, may hold values from -2 to 2
- track_offsets: int32 [4, 32], replicated, may hold values from 0 to 63
Outputs:
- despeckled: float32 [8192, 4096], P('sub', 'rng')
The draws below stay inside these ranges and needn't reach their ends.
All inputs are finite; a program needn't handle non-finite values.
Results may differ from the reference program's by a relative error of at most 0.0045.
Values may be sent and summed in bfloat16 or wider, within the bound.
A program may use at most 64 MiB of HBM per device.

```python
import math
import jax
import jax.numpy as jnp
import numpy as np
from jax import lax

FACTOR = 64
ANG = 256
TAPS = 8
MERGES = 4
SWEEPS = 8
SAMPLES = 4096
PULSES = 32768
N_SUB = 32


def plant(entries, key, smallest, largest):
    longest = entries.shape.index(max(entries.shape))
    spots = []
    for shift in (0, 1):
        where = [jax.random.randint(jax.random.fold_in(key, axis), (), 0, length) for axis, length in enumerate(entries.shape)]
        where[longest] = (where[longest] + shift) % entries.shape[longest]
        spots.append(tuple(where))
    return entries.at[spots[0]].set(smallest).at[spots[1]].set(largest)


def levels(stream_key, extent, split, least, high):
    gain, own = 1.0, jax.random.fold_in(stream_key, 6)
    for position, blocks in split:
        draws = jnp.exp(jax.random.uniform(jax.random.fold_in(own, position), (blocks,), jnp.float32, least / len(split), high / len(split)))
        gain = gain * jnp.repeat(draws, extent[position] // blocks).reshape([-1 if axis == position else 1 for axis in range(len(extent))])
    return gain


def bell_draw(stream_key, shape, width, most, pieces=(), held_as=jnp.bfloat16):
    entries = jax.random.normal(stream_key, shape, jnp.float32) * width
    if len(pieces) > 0:
        entries = levels(stream_key, shape, pieces, -0.22, 0.18) * entries
    return jnp.clip(entries, min=-most, max=most).astype(held_as)


def setup_inputs(seed: int = 0) -> dict:
    keys = jax.random.split(jax.random.key(seed), 5)
    return {
        "raw_echoes": bell_draw(keys[0], (2, PULSES, SAMPLES), 1.0, 6.0, ((1, 256),)),
        "merge_taps": plant(jax.random.randint(keys[1], (MERGES, 2, TAPS, 2 * ANG), 0, ANG), jax.random.fold_in(keys[1], 1), 0, ANG - 1).astype(jnp.int32),
        "merge_weights": bell_draw(keys[2], (MERGES, 2, TAPS, 2 * ANG), TAPS ** -0.5, 2.0, (), jnp.float32),
        "track_offsets": plant(jax.random.randint(keys[3], (MERGES, N_SUB), 0, 64), jax.random.fold_in(keys[3], 1), 0, 63).astype(jnp.int32),
    }


inv_root_two = 0.7071067811865476
diffusion_rate = 0.5
edge_scale = 2.0
phase_period = 8192

def complex_mix(real_in, imag_in, cosine_table, sine_table, form):
    highest = lax.Precision.HIGHEST
    real_out = jnp.einsum(form, real_in, cosine_table, precision=highest) + jnp.einsum(form, imag_in, sine_table, precision=highest)
    imag_out = jnp.einsum(form, imag_in, cosine_table, precision=highest) - jnp.einsum(form, real_in, sine_table, precision=highest)
    return (real_out, imag_out)

def range_transform(raw_block, factor):
    row_count = raw_block.shape[1]
    samples_all = factor * factor
    samples_in = raw_block.astype(jnp.float32).reshape(2, row_count, factor, factor)
    sample_index = jnp.arange(factor, dtype=jnp.int32)
    product = sample_index[:, None] * sample_index[None, :]
    coarse = 2.0 * math.pi / factor * (product % factor).astype(jnp.float32)
    twiddle = 2.0 * math.pi / samples_all * (product % samples_all).astype(jnp.float32)
    cosine_table = jnp.cos(coarse)
    sine_table = jnp.sin(coarse)
    first_real, first_imag = complex_mix(samples_in[0], samples_in[1], cosine_table, sine_table, 'pab,ac->pbc')
    twist_cos = jnp.cos(twiddle)
    twist_sin = jnp.sin(twiddle)
    second_real = first_real * twist_cos + first_imag * twist_sin
    second_imag = first_imag * twist_cos - first_real * twist_sin
    final_real, final_imag = complex_mix(second_real, second_imag, cosine_table, sine_table, 'pbc,bd->pdc')
    norm_scale = 1.0 / factor
    return jnp.stack([final_real, final_imag]).reshape(2, row_count, samples_all) * norm_scale

def beam_tables(angle_count, leaf_pulses):
    angle_index = jnp.arange(angle_count, dtype=jnp.int32) - angle_count // 2
    pulse_index = jnp.arange(leaf_pulses, dtype=jnp.int32)
    wrapped = angle_index[:, None] * pulse_index[None, :] % leaf_pulses
    angles_now = 2.0 * math.pi / leaf_pulses * wrapped.astype(jnp.float32)
    norm_scale = 1.0 / math.sqrt(leaf_pulses)
    return ((jnp.cos(angles_now) * norm_scale).astype(jnp.bfloat16), (jnp.sin(angles_now) * norm_scale).astype(jnp.bfloat16))

def form_leaf(compressed, cosine_table, sine_table):
    real_part = jnp.dot(cosine_table, compressed[0], preferred_element_type=jnp.float32) + jnp.dot(sine_table, compressed[1], preferred_element_type=jnp.float32)
    imag_part = jnp.dot(cosine_table, compressed[1], preferred_element_type=jnp.float32) - jnp.dot(sine_table, compressed[0], preferred_element_type=jnp.float32)
    return jnp.stack([real_part, imag_part]).astype(jnp.bfloat16)

def interp_matrix(taps_rows, weights_rows, angle_count):
    columns = jnp.arange(angle_count, dtype=jnp.int32)
    summed = jnp.zeros((taps_rows.shape[1], angle_count), jnp.float32)
    for tap_index in range(taps_rows.shape[0]):
        summed = summed + jnp.where(taps_rows[tap_index][:, None] == columns[None, :], weights_rows[tap_index][:, None], 0.0)
    return summed.astype(jnp.bfloat16)

def contribute(sector_image, matrix, offset, row_anchor, col_anchor):
    proj_real = jnp.dot(matrix, sector_image[0], preferred_element_type=jnp.float32)
    proj_imag = jnp.dot(matrix, sector_image[1], preferred_element_type=jnp.float32)
    row_index = row_anchor + jnp.arange(matrix.shape[0], dtype=jnp.int32)
    col_index = col_anchor + 1 + jnp.arange(sector_image.shape[2], dtype=jnp.int32)
    wrapped = (offset * row_index % phase_period)[:, None] * col_index[None, :] % phase_period
    motion_phase = 2.0 * math.pi / phase_period * wrapped.astype(jnp.float32)
    cosine_now = jnp.cos(motion_phase)
    sine_now = jnp.sin(motion_phase)
    return jnp.stack([proj_real * cosine_now - proj_imag * sine_now, proj_real * sine_now + proj_imag * cosine_now])

def conduct(difference):
    scaled = difference / edge_scale
    return 1.0 / (1.0 + scaled * scaled)

def diffuse(padded):
    center = padded[:, 1:-1]
    upper_diff = padded[:, 2:] - center
    lower_diff = center - padded[:, :-2]
    return center + diffusion_rate * (conduct(upper_diff) * upper_diff - conduct(lower_diff) * lower_diff)

def reference(raw_echoes, merge_taps, merge_weights, track_offsets):
    leaf_pulses = raw_echoes.shape[1] // N_SUB
    cosine_table, sine_table = beam_tables(ANG, leaf_pulses)

    def leaf_one(block_index):
        block = lax.dynamic_slice_in_dim(raw_echoes, (block_index * leaf_pulses).astype(jnp.int32), leaf_pulses, 1)
        compressed = range_transform(block, FACTOR).astype(jnp.bfloat16)
        return form_leaf(compressed, cosine_table, sine_table)
    images = lax.map(leaf_one, jnp.arange(N_SUB, dtype=jnp.int32))
    leaves = np.arange(N_SUB)
    sectors = np.zeros(N_SUB, dtype=np.int64)
    for merge_level in range(MERGES):
        partner_bit = 1 << merge_level
        sides = leaves >> merge_level & 1
        matrices = jnp.stack([interp_matrix(merge_taps[merge_level, half], merge_weights[merge_level, half], ANG) for half in range(2)])

        def part_one(items):
            sector_image, half_bit, offset, sector_now = items
            return contribute(sector_image, matrices[half_bit], offset, sector_now * (2 * ANG), jnp.int32(0))
        parts = lax.map(part_one, (images, jnp.asarray(sides, dtype=jnp.int32), track_offsets[merge_level], jnp.asarray(sectors, dtype=jnp.int32)))
        halves = parts.reshape(N_SUB, 2, 2, ANG, SAMPLES)
        own_half = halves[leaves, :, sides]
        partner_half = halves[leaves ^ partner_bit, :, sides]
        images = ((own_half + partner_half) * inv_root_two).astype(jnp.bfloat16)
        sectors = sectors * 2 + sides
    real_part = images[:, 0].astype(jnp.float32)
    imag_part = images[:, 1].astype(jnp.float32)
    intensity = jnp.sqrt(real_part * real_part + imag_part * imag_part).reshape(N_SUB * ANG, SAMPLES)
    for sweep_index in range(SWEEPS):
        padded = jnp.pad(intensity, ((0, 0), (1, 1)), mode='symmetric')
        intensity = diffuse(padded)
    return intensity
```

```python
import functools
import math

import jax
import jax.numpy as jnp
import numpy as np
from jax import lax
from jax.experimental import pallas as pl
from jax.experimental.pallas import tpu as pltpu
from jax.sharding import PartitionSpec as P

FACTOR = 64
ANG = 256
TAPS = 8
MERGES = 4
SWEEPS = 8
PERIOD = 8192
LANES = 128
CHUNKS = 4
GROUPS = 8
MESH = pl.DeviceIdType.MESH

bf16 = jnp.bfloat16
f32 = jnp.float32


def make_tables():
    tile = np.arange(LANES)
    b = np.arange(LANES)
    second = np.zeros((GROUPS, 2, LANES, 2, LANES))
    for g in range(GROUPS):
        r = (tile // 16 - g) % 8
        d = 16 * r + tile % 16
        angle = 2.0 * np.pi / 128.0 * ((b[:, None] * d[None, :]) % 128)
        cosine, sine = np.cos(angle) / FACTOR, np.sin(angle) / FACTOR
        second[g, 0, :, 0] = cosine
        second[g, 1, :, 0] = sine
        second[g, 0, :, 1] = -sine
        second[g, 1, :, 1] = cosine
    second = second.reshape(GROUPS, 2 * LANES, 2 * LANES)
    c = np.arange(32)
    angle = 2.0 * np.pi / 4096.0 * (c[:, None] * b[None, :])
    twiddle = np.stack([np.cos(angle), np.sin(angle)])
    a = np.arange(ANG) - ANG // 2
    q = np.arange(1024)
    angle = 2.0 * np.pi / 1024.0 * ((a[:, None] * q[None, :]) % 1024)
    beam = np.stack([np.cos(angle), np.sin(angle)]) / 32.0
    beam = beam.reshape(2, ANG, 4, 2, LANES).transpose(3, 0, 1, 2, 4)
    return (
        second.astype(jnp.bfloat16),
        twiddle.astype(np.float32),
        np.ascontiguousarray(beam).astype(jnp.bfloat16),
    )


def transform_eight(z):
    half = math.sqrt(0.5)

    def four(v):
        (ar, ai), (br, bi), (cr, ci), (dr, di) = v
        sr, si, tr, ti = ar + cr, ai + ci, ar - cr, ai - ci
        ur, ui, vr, vi = br + dr, bi + di, br - dr, bi - di
        return [(sr + ur, si + ui), (tr + vi, ti - vr), (sr - ur, si - ui), (tr - vi, ti + vr)]

    even = four(z[0::2])
    odd = four(z[1::2])
    (o0r, o0i), (o1r, o1i), (o2r, o2i), (o3r, o3i) = odd
    turned = [
        (o0r, o0i),
        ((o1r + o1i) * half, (o1i - o1r) * half),
        (o2i, -o2r),
        ((o3i - o3r) * half, (-o3i - o3r) * half),
    ]
    low = [(er + tr, ei + ti) for (er, ei), (tr, ti) in zip(even, turned)]
    high = [(er - tr, ei - ti) for (er, ei), (tr, ti) in zip(even, turned)]
    return low + high


def unit_circle(steps):
    moved = steps + 1024
    quadrant = moved >> 11
    x = ((moved & 2047) - 1024).astype(f32) * (2.0 * math.pi / PERIOD)
    z = x * x
    sine = x * (1.0 + z * (-1.0 / 6.0 + z * (1.0 / 120.0 - z * (1.0 / 5040.0))))
    cosine = 1.0 + z * (-0.5 + z * (1.0 / 24.0 + z * (-1.0 / 720.0 + z * (1.0 / 40320.0))))
    swap = (quadrant & 1) == 1
    out_cos = jnp.where(swap, sine, cosine)
    out_sin = jnp.where(swap, cosine, sine)
    out_cos = jnp.where(((quadrant + 1) & 2) == 2, -out_cos, out_cos)
    out_sin = jnp.where((quadrant & 2) == 2, -out_sin, out_sin)
    return out_cos, out_sin


def order_of_steps():
    return [
        ("beam", 0), ("lead", 0), ("m0", 0), ("beam", 1), ("m1", 0), ("lead", 1), ("m0", 1),
        ("m2", 0), ("beam", 2), ("m1", 1), ("lead", 2), ("m0", 2), ("m2", 1), ("m3", 0), ("beam", 3),
        ("m1", 2), ("lead", 3), ("m0", 3), ("m2", 2), ("m3", 1), ("m1", 3), ("m2", 3), ("m3", 2), ("m3", 3),
    ]


def kernel(
    raw_hbm, second_hbm, beam_hbm, twiddle_ref, taps_ref, weights_ref, offsets_ref, out_ref,
    raw, second, beam, left, rows_buf, wide, sent, got, part_out, part_in, part_own,
    image, image_in, own_part, phase, mats, perm, final, halo_out, halo_in,
    in_sem, own_sem, send_a, recv_a, send_x, recv_x, send_m, recv_m, send_h, recv_h,
):
    sub = lax.axis_index("sub")
    rng = lax.axis_index("rng")
    x_lo = rng % 2
    y = rng // 2

    half_bits = [(sub // 2**l) % 2 for l in range(MERGES)]
    partners = [sub + 2**l - 2 * 2**l * half_bits[l] for l in range(MERGES)]
    x_partner = rng + 1 - 2 * x_lo
    y_partners = [((y + j) % 4) * 2 + x_lo for j in (1, 2, 3)]
    halo_partners = [(rng + 7) % 8, (rng + 1) % 8]

    raw_copies = [
        pltpu.make_async_copy(raw_hbm.at[:, pl.ds(64 * h, 64)], raw.at[:, pl.ds(64 * h, 64)], in_sem.at[h])
        for h in range(2)
    ]
    second_copy = pltpu.make_async_copy(second_hbm, second, in_sem.at[2])
    beam_copy = pltpu.make_async_copy(beam_hbm.at[x_lo], beam, in_sem.at[3])
    for copy in raw_copies:
        copy.start()
    second_copy.start()
    beam_copy.start()

    barrier = pltpu.get_barrier_semaphore()
    ids = [{"rng": t} for t in y_partners + [x_partner] + halo_partners] + [{"sub": t} for t in partners]
    for one in ids:
        pl.semaphore_signal(barrier, inc=1, device_id=one, device_id_type=MESH)

    lane = lax.broadcasted_iota(jnp.int32, (16, LANES), 1)
    group_bits = [((lane // 16) // 2**t) % 2 == 1 for t in range(3)]
    a_copies = {}
    own_copies = {}

    def transform(i, first):
        def rows(block, carry):
            at = pl.ds(pl.multiple_of(block * 16, 16), 16)

            def load(part, a):
                return raw[part, at, a * LANES : (a + 1) * LANES].astype(f32)

            mixed = []
            for m in range(8):
                v = [(load(0, m + 8 * j), load(1, m + 8 * j)) for j in range(4)]
                if i % 2 == 0:
                    sr, si = v[0][0] + v[2][0], v[0][1] + v[2][1]
                    tr, ti = v[1][0] + v[3][0], v[1][1] + v[3][1]
                    zr, zi = (sr + tr, si + ti) if i == 0 else (sr - tr, si - ti)
                else:
                    sr, si = v[0][0] - v[2][0], v[0][1] - v[2][1]
                    tr, ti = v[1][0] - v[3][0], v[1][1] - v[3][1]
                    zr, zi = (sr + ti, si - tr) if i == 1 else (sr - ti, si + tr)
                if i * m:
                    turn = 2.0 * math.pi * i * m / 32.0
                    wc, ws = math.cos(turn), math.sin(turn)
                    zr, zi = zr * wc + zi * ws, zi * wc - zr * ws
                mixed.append((zr, zi))
            for g, (zr, zi) in enumerate(transform_eight(mixed)):
                c = i + 4 * g
                wc = twiddle_ref[0, c : c + 1, :]
                ws = twiddle_ref[1, c : c + 1, :]
                rows_buf[g, at, 0:LANES] = (zr * wc + zi * ws).astype(bf16)
                rows_buf[g, at, LANES : 2 * LANES] = (zi * wc - zr * ws).astype(bf16)
            return carry

        if first:
            raw_copies[0].wait()
            lax.fori_loop(0, 4, rows, 0)
            raw_copies[1].wait()
            lax.fori_loop(4, 8, rows, 0)
            second_copy.wait()
        else:
            lax.fori_loop(0, 8, rows, 0)
        for g in range(GROUPS):
            wide[g] = jnp.dot(rows_buf[g], second[g], preferred_element_type=f32)

        def pick(block, carry):
            at = pl.ds(pl.multiple_of(block * 16, 16), 16)
            for part in range(2):
                tiles = [wide[(8 - r) % 8, at, part * LANES : (part + 1) * LANES] for r in range(8)]
                for t in range(3):
                    tiles = [jnp.where(group_bits[t], tiles[(r - 2**t) % 8], tiles[r]) for r in range(8)]
                for r in range(8):
                    sent[i, r // 2, part, at, (r % 2) * LANES : (r % 2 + 1) * LANES] = tiles[r].astype(bf16)
            return carry

        lax.fori_loop(0, 8, pick, 0)
        if first:
            pl.semaphore_wait(barrier, len(ids))
        for j in (2, 1, 3):
            target = (y + j) % 4
            copy = pltpu.make_async_remote_copy(
                src_ref=sent.at[i, target],
                dst_ref=got.at[i, y],
                send_sem=send_a.at[i, j - 1],
                recv_sem=recv_a.at[i, j - 1],
                device_id={"rng": target * 2 + x_lo},
                device_id_type=MESH,
            )
            copy.start()
            a_copies[i, j] = copy
        own_copies[i] = pltpu.make_async_copy(sent.at[i, y], got.at[i, y], own_sem.at[i])
        own_copies[i].start()

    for i in range(CHUNKS):
        transform(i, i == 0)

    beam_copy.wait()
    for t in range(4):
        cosine, sine = beam[0, :, t], beam[1, :, t]
        left[0:ANG, (2 * t) * LANES : (2 * t + 1) * LANES] = cosine
        left[0:ANG, (2 * t + 1) * LANES : (2 * t + 2) * LANES] = sine
        left[ANG:, (2 * t) * LANES : (2 * t + 1) * LANES] = -sine
        left[ANG:, (2 * t + 1) * LANES : (2 * t + 2) * LANES] = cosine

    angle_rows = lax.broadcasted_iota(jnp.int32, (ANG, ANG), 0)
    sector = sub * 0
    for l in range(MERGES):
        bit = half_bits[l]
        for which in range(2):
            half = bit if which == 0 else 1 - bit
            at = pl.ds(pl.multiple_of(bit * ANG, ANG), ANG)
            taps = taps_ref[l, half, :, at]
            weights = weights_ref[l, half, :, at]
            total = jnp.zeros((ANG, ANG), f32)
            for t in range(TAPS):
                total = total + jnp.where(taps[t : t + 1, :] == angle_rows, weights[t : t + 1, :], 0.0)
            mats[l, which] = total.T.astype(bf16)
            offset = offsets_ref[l, sub] if which == 0 else offsets_ref[l, partners[l]]
            anchor = sector * (2 * ANG) + bit * ANG

            def fill(block, carry, l=l, which=which, offset=offset, anchor=anchor):
                start = pl.multiple_of(block * 32, 32)
                at = pl.ds(start, 32)
                row = lax.broadcasted_iota(jnp.int32, (32, LANES), 0)
                col = lax.broadcasted_iota(jnp.int32, (32, LANES), 1)
                column = 512 * rng + 32 * (col & 15) + 4 * (((col >> 4) - rng) & 7) + 1
                slope = (offset * (anchor + start + row)) & (PERIOD - 1)
                er, ei = unit_circle((slope * column) & (PERIOD - 1))
                tr, ti = unit_circle(slope)
                er, ei = er * 0.7071067811865476, ei * 0.7071067811865476
                for i in range(CHUNKS):
                    phase[l, which, i, 0, at] = er
                    phase[l, which, i, 1, at] = ei
                    if i < CHUNKS - 1:
                        er, ei = er * tr - ei * ti, er * ti + ei * tr
                return carry

            lax.fori_loop(0, ANG // 32, fill, 0)
        sector = sector * 2 + bit

    for i in range(CHUNKS):
        from_lane = lax.broadcasted_iota(jnp.int32, (LANES, 512), 0)
        to_lane = lax.broadcasted_iota(jnp.int32, (LANES, 512), 1)
        place = 32 * (from_lane & 15) + 4 * (((from_lane >> 4) - rng) & 7) + i
        perm[i * LANES : (i + 1) * LANES, :] = jnp.where(place == to_lane, 1.0, 0.0).astype(bf16)

    x_copies = {}
    m_copies = {}

    def contribution(l, which, i, ref):
        both = jnp.concatenate([ref[0], ref[1]], axis=1)
        proj = jnp.dot(mats[l, which], both, preferred_element_type=f32)
        pr, pi = proj[:, :LANES], proj[:, LANES:]
        er, ei = phase[l, which, i, 0], phase[l, which, i, 1]
        return pr * er - pi * ei, pr * ei + pi * er

    def pass_on(l, i):
        copy = pltpu.make_async_remote_copy(
            src_ref=image.at[l, i],
            dst_ref=image_in.at[l, i],
            send_sem=send_m.at[l, i],
            recv_sem=recv_m.at[l, i],
            device_id={"sub": partners[l]},
            device_id_type=MESH,
        )
        copy.start()
        m_copies[l, i] = copy
        re, im = contribution(l, 0, i, image.at[l, i])
        own_part[l, i, 0] = re
        own_part[l, i, 1] = im

    def step(kind, i):
        if kind == "beam":
            for j in (1, 2, 3):
                a_copies[i, j].wait_recv()
            own_copies[i].wait()
            total = jnp.dot(left[...], got[i].reshape(1024, 2 * LANES), preferred_element_type=f32)
            low, high = total[:, :LANES], total[:, LANES:]
            is_low = x_lo == 0
            part_out[i] = jnp.where(is_low, high, low).astype(bf16)
            copy = pltpu.make_async_remote_copy(
                src_ref=part_out.at[i],
                dst_ref=part_in.at[i],
                send_sem=send_x.at[i],
                recv_sem=recv_x.at[i],
                device_id={"rng": x_partner},
                device_id_type=MESH,
            )
            copy.start()
            x_copies[i] = copy
            part_own[i] = jnp.where(is_low, low, high)
        elif kind == "lead":
            x_copies[i].wait_recv()
            total = (part_own[i] + part_in[i].astype(f32)).astype(bf16)
            image[0, i, 0] = total[:ANG]
            image[0, i, 1] = total[ANG:]
            pass_on(0, i)
        else:
            l = int(kind[1])
            m_copies[l, i].wait_recv()
            re, im = contribution(l, 1, i, image_in.at[l, i])
            re = (re + own_part[l, i, 0]).astype(bf16)
            im = (im + own_part[l, i, 1]).astype(bf16)
            if l < MERGES - 1:
                image[l + 1, i, 0] = re
                image[l + 1, i, 1] = im
                pass_on(l + 1, i)
            else:
                final[0, :, i * LANES : (i + 1) * LANES] = re
                final[1, :, i * LANES : (i + 1) * LANES] = im

    for kind, i in order_of_steps():
        step(kind, i)

    re = jnp.dot(final[0], perm[...], preferred_element_type=f32)
    im = jnp.dot(final[1], perm[...], preferred_element_type=f32)
    out_ref[...] = jnp.sqrt(re * re + im * im)
    halo_out[0] = out_ref[:, 0:LANES].astype(bf16)
    halo_out[1] = out_ref[:, 512 - LANES : 512].astype(bf16)
    halo_copies = []
    for side in range(2):
        copy = pltpu.make_async_remote_copy(
            src_ref=halo_out.at[side],
            dst_ref=halo_in.at[side],
            send_sem=send_h.at[side],
            recv_sem=recv_h.at[side],
            device_id={"rng": halo_partners[side]},
            device_id_type=MESH,
        )
        copy.start()
        halo_copies.append(copy)
    for copy in halo_copies:
        copy.wait_recv()

    ring = 512 + LANES
    spot = lax.broadcasted_iota(jnp.int32, (16, ring), 1)
    closed = ((spot == ring - 1) & (rng == 0)) | ((spot == 511) & (rng == 7))
    rate = jnp.where(closed, 0.0, 0.5)
    side_lane = lax.broadcasted_iota(jnp.int32, (16, LANES), 1)

    def spread(block, carry):
        at = pl.ds(pl.multiple_of(block * 16, 16), 16)
        edge = jnp.where(side_lane < LANES // 2, halo_in[0, at].astype(f32), halo_in[1, at].astype(f32))
        u = jnp.concatenate([out_ref[at, :], edge], axis=1)
        for sweep in range(SWEEPS):
            diff = pltpu.roll(u, ring - 1, 1) - u
            flux = diff * rate / (1.0 + 0.25 * (diff * diff))
            u = u + (flux - pltpu.roll(flux, 1, 1))
        out_ref[at, :] = u[:, :512]
        return carry

    lax.fori_loop(0, ANG // 16, spread, 0)

    for copy in list(a_copies.values()) + list(x_copies.values()) + list(m_copies.values()) + halo_copies:
        copy.wait_send()


def per_device(raw_echoes, merge_taps, merge_weights, track_offsets):
    second, twiddle, beam = make_tables()
    vmem = pl.BlockSpec(memory_space=pltpu.VMEM)
    smem = pl.BlockSpec(memory_space=pltpu.SMEM)
    anywhere = pl.BlockSpec(memory_space=pl.ANY)
    dma = pltpu.SemaphoreType.DMA
    return pl.pallas_call(
        kernel,
        out_shape=jax.ShapeDtypeStruct((ANG, 512), f32),
        in_specs=[anywhere, anywhere, anywhere, vmem, vmem, vmem, smem],
        out_specs=vmem,
        scratch_shapes=[
            pltpu.VMEM((2, 128, 4096), bf16),
            pltpu.VMEM((GROUPS, 256, 256), bf16),
            pltpu.VMEM((2, ANG, 4, LANES), bf16),
            pltpu.VMEM((2 * ANG, 1024), bf16),
            pltpu.VMEM((GROUPS, 128, 256), bf16),
            pltpu.VMEM((GROUPS, 128, 256), f32),
            pltpu.VMEM((CHUNKS, 4, 2, 128, 2 * LANES), bf16),
            pltpu.VMEM((CHUNKS, 4, 2, 128, 2 * LANES), bf16),
            pltpu.VMEM((CHUNKS, 2 * ANG, LANES), bf16),
            pltpu.VMEM((CHUNKS, 2 * ANG, LANES), bf16),
            pltpu.VMEM((CHUNKS, 2 * ANG, LANES), f32),
            pltpu.VMEM((MERGES, CHUNKS, 2, ANG, LANES), bf16),
            pltpu.VMEM((MERGES, CHUNKS, 2, ANG, LANES), bf16),
            pltpu.VMEM((MERGES, CHUNKS, 2, ANG, LANES), f32),
            pltpu.VMEM((MERGES, 2, CHUNKS, 2, ANG, LANES), f32),
            pltpu.VMEM((MERGES, 2, ANG, ANG), bf16),
            pltpu.VMEM((512, 512), bf16),
            pltpu.VMEM((2, ANG, 512), bf16),
            pltpu.VMEM((2, ANG, LANES), bf16),
            pltpu.VMEM((2, ANG, LANES), bf16),
            dma((4,)),
            dma((CHUNKS,)),
            dma((CHUNKS, 3)),
            dma((CHUNKS, 3)),
            dma((CHUNKS,)),
            dma((CHUNKS,)),
            dma((MERGES, CHUNKS)),
            dma((MERGES, CHUNKS)),
            dma((2,)),
            dma((2,)),
        ],
        compiler_params=pltpu.CompilerParams(
            collective_id=0, has_side_effects=True, vmem_limit_bytes=56 << 20
        ),
        name="backproject",
    )(
        raw_echoes,
        jnp.asarray(second),
        jnp.asarray(beam),
        jnp.asarray(twiddle),
        merge_taps,
        merge_weights,
        track_offsets,
    )


def solution(mesh):
    in_specs = (P(None, ("sub", "rng"), None), P(), P(), P())
    out_specs = P("sub", "rng")
    return jax.shard_map(
        per_device, mesh=mesh, in_specs=in_specs, out_specs=out_specs, check_vma=False
    )
```

```python
import functools
import math

import jax
import jax.numpy as jnp
import numpy as np
from jax import lax
from jax.experimental import pallas as pl
from jax.experimental.pallas import tpu as pltpu
from jax.sharding import PartitionSpec as P

FACTOR = 64
ANG = 256
TAPS = 8
MERGES = 4
SWEEPS = 8
PERIOD = 8192
LANES = 128
CHUNKS = 4
GROUPS = 8
MESH = pl.DeviceIdType.MESH

bf16 = jnp.bfloat16
f32 = jnp.float32


def make_tables():
    tile = np.arange(LANES)
    b = np.arange(LANES)
    second = np.zeros((GROUPS, 2, LANES, 2, LANES))
    for g in range(GROUPS):
        r = (tile // 16 - g) % 8
        d = 16 * r + tile % 16
        angle = 2.0 * np.pi / 128.0 * ((b[:, None] * d[None, :]) % 128)
        cosine, sine = np.cos(angle) / FACTOR, np.sin(angle) / FACTOR
        second[g, 0, :, 0] = cosine
        second[g, 1, :, 0] = sine
        second[g, 0, :, 1] = -sine
        second[g, 1, :, 1] = cosine
    second = second.reshape(GROUPS, 2 * LANES, 2 * LANES)
    c = np.arange(32)
    angle = 2.0 * np.pi / 4096.0 * (c[:, None] * b[None, :])
    twiddle = np.stack([np.cos(angle), np.sin(angle)])
    a = np.arange(ANG) - ANG // 2
    q = np.arange(1024)
    angle = 2.0 * np.pi / 1024.0 * ((a[:, None] * q[None, :]) % 1024)
    beam = np.stack([np.cos(angle), np.sin(angle)]) / 32.0
    beam = beam.reshape(2, ANG, 4, 2, LANES).transpose(3, 0, 1, 2, 4)
    return (
        second.astype(jnp.bfloat16),
        twiddle.astype(np.float32),
        np.ascontiguousarray(beam).astype(jnp.bfloat16),
    )


def transform_eight(z):
    half = math.sqrt(0.5)

    def four(v):
        (ar, ai), (br, bi), (cr, ci), (dr, di) = v
        sr, si, tr, ti = ar + cr, ai + ci, ar - cr, ai - ci
        ur, ui, vr, vi = br + dr, bi + di, br - dr, bi - di
        return [(sr + ur, si + ui), (tr + vi, ti - vr), (sr - ur, si - ui), (tr - vi, ti + vr)]

    even = four(z[0::2])
    odd = four(z[1::2])
    (o0r, o0i), (o1r, o1i), (o2r, o2i), (o3r, o3i) = odd
    turned = [
        (o0r, o0i),
        ((o1r + o1i) * half, (o1i - o1r) * half),
        (o2i, -o2r),
        ((o3i - o3r) * half, (-o3i - o3r) * half),
    ]
    low = [(er + tr, ei + ti) for (er, ei), (tr, ti) in zip(even, turned)]
    high = [(er - tr, ei - ti) for (er, ei), (tr, ti) in zip(even, turned)]
    return low + high


def unit_circle(steps):
    moved = steps + 1024
    quadrant = moved >> 11
    x = ((moved & 2047) - 1024).astype(f32) * (2.0 * math.pi / PERIOD)
    z = x * x
    sine = x * (1.0 + z * (-1.0 / 6.0 + z * (1.0 / 120.0 - z * (1.0 / 5040.0))))
    cosine = 1.0 + z * (-0.5 + z * (1.0 / 24.0 + z * (-1.0 / 720.0 + z * (1.0 / 40320.0))))
    swap = (quadrant & 1) == 1
    out_cos = jnp.where(swap, sine, cosine)
    out_sin = jnp.where(swap, cosine, sine)
    out_cos = jnp.where(((quadrant + 1) & 2) == 2, -out_cos, out_cos)
    out_sin = jnp.where((quadrant & 2) == 2, -out_sin, out_sin)
    return out_cos, out_sin


def order_of_steps():
    return [
        ("beam", 0), ("lead", 0), ("m0", 0), ("beam", 1), ("m1", 0), ("lead", 1), ("m0", 1),
        ("m2", 0), ("beam", 2), ("m1", 1), ("lead", 2), ("m0", 2), ("m2", 1), ("m3", 0), ("beam", 3),
        ("m1", 2), ("lead", 3), ("m0", 3), ("m2", 2), ("m3", 1), ("m1", 3), ("m2", 3), ("m3", 2), ("m3", 3),
    ]


def kernel(
    raw_hbm, second_hbm, beam_hbm, twiddle_ref, taps_ref, weights_ref, offsets_ref, out_ref,
    raw, second, beam, left, rows_buf, wide, sent, got, part_out, part_in, part_own,
    image, image_in, own_part, phase, mats, perm, final, level, smooth, halo_out, halo_in,
    in_sem, own_sem, send_a, recv_a, send_x, recv_x, send_m, recv_m, send_h, recv_h,
):
    sub = lax.axis_index("sub")
    rng = lax.axis_index("rng")
    x_lo = rng % 2
    y = rng // 2

    half_bits = [(sub // 2**l) % 2 for l in range(MERGES)]
    partners = [sub + 2**l - 2 * 2**l * half_bits[l] for l in range(MERGES)]
    x_partner = rng + 1 - 2 * x_lo
    y_partners = [((y + j) % 4) * 2 + x_lo for j in (1, 2, 3)]
    halo_partners = [(rng + 7) % 8, (rng + 1) % 8]

    raw_copies = [
        pltpu.make_async_copy(raw_hbm.at[:, pl.ds(64 * h, 64)], raw.at[:, pl.ds(64 * h, 64)], in_sem.at[h])
        for h in range(2)
    ]
    second_copy = pltpu.make_async_copy(second_hbm, second, in_sem.at[2])
    beam_copy = pltpu.make_async_copy(beam_hbm.at[x_lo], beam, in_sem.at[3])
    for copy in raw_copies:
        copy.start()
    second_copy.start()
    beam_copy.start()

    barrier = pltpu.get_barrier_semaphore()
    ids = [{"rng": t} for t in y_partners + [x_partner] + halo_partners] + [{"sub": t} for t in partners]
    for one in ids:
        pl.semaphore_signal(barrier, inc=1, device_id=one, device_id_type=MESH)

    lane = lax.broadcasted_iota(jnp.int32, (16, LANES), 1)
    group_bits = [((lane // 16) // 2**t) % 2 == 1 for t in range(3)]
    a_copies = {}
    own_copies = {}

    def transform(i, first):
        def rows(block, carry):
            at = pl.ds(pl.multiple_of(block * 16, 16), 16)

            def load(part, a):
                return raw[part, at, a * LANES : (a + 1) * LANES].astype(f32)

            mixed = []
            for m in range(8):
                v = [(load(0, m + 8 * j), load(1, m + 8 * j)) for j in range(4)]
                if i % 2 == 0:
                    sr, si = v[0][0] + v[2][0], v[0][1] + v[2][1]
                    tr, ti = v[1][0] + v[3][0], v[1][1] + v[3][1]
                    zr, zi = (sr + tr, si + ti) if i == 0 else (sr - tr, si - ti)
                else:
                    sr, si = v[0][0] - v[2][0], v[0][1] - v[2][1]
                    tr, ti = v[1][0] - v[3][0], v[1][1] - v[3][1]
                    zr, zi = (sr + ti, si - tr) if i == 1 else (sr - ti, si + tr)
                if i * m:
                    turn = 2.0 * math.pi * i * m / 32.0
                    wc, ws = math.cos(turn), math.sin(turn)
                    zr, zi = zr * wc + zi * ws, zi * wc - zr * ws
                mixed.append((zr, zi))
            for g, (zr, zi) in enumerate(transform_eight(mixed)):
                c = i + 4 * g
                wc = twiddle_ref[0, c : c + 1, :]
                ws = twiddle_ref[1, c : c + 1, :]
                rows_buf[g, at, 0:LANES] = (zr * wc + zi * ws).astype(bf16)
                rows_buf[g, at, LANES : 2 * LANES] = (zi * wc - zr * ws).astype(bf16)
            return carry

        if first:
            raw_copies[0].wait()
            lax.fori_loop(0, 4, rows, 0)
            raw_copies[1].wait()
            lax.fori_loop(4, 8, rows, 0)
            second_copy.wait()
        else:
            lax.fori_loop(0, 8, rows, 0)
        for g in range(GROUPS):
            wide[g] = jnp.dot(rows_buf[g], second[g], preferred_element_type=f32)

        def pick(block, carry):
            at = pl.ds(pl.multiple_of(block * 16, 16), 16)
            for part in range(2):
                tiles = [wide[(8 - r) % 8, at, part * LANES : (part + 1) * LANES] for r in range(8)]
                for t in range(3):
                    tiles = [jnp.where(group_bits[t], tiles[(r - 2**t) % 8], tiles[r]) for r in range(8)]
                for r in range(8):
                    sent[i, r // 2, part, at, (r % 2) * LANES : (r % 2 + 1) * LANES] = tiles[r].astype(bf16)
            return carry

        lax.fori_loop(0, 8, pick, 0)
        if first:
            pl.semaphore_wait(barrier, len(ids))
        for j in (2, 1, 3):
            target = (y + j) % 4
            copy = pltpu.make_async_remote_copy(
                src_ref=sent.at[i, target],
                dst_ref=got.at[i, y],
                send_sem=send_a.at[i, j - 1],
                recv_sem=recv_a.at[i, j - 1],
                device_id={"rng": target * 2 + x_lo},
                device_id_type=MESH,
            )
            copy.start()
            a_copies[i, j] = copy
        own_copies[i] = pltpu.make_async_copy(sent.at[i, y], got.at[i, y], own_sem.at[i])
        own_copies[i].start()

    for i in range(CHUNKS):
        transform(i, i == 0)

    beam_copy.wait()
    for t in range(4):
        cosine, sine = beam[0, :, t], beam[1, :, t]
        left[0:ANG, (2 * t) * LANES : (2 * t + 1) * LANES] = cosine
        left[0:ANG, (2 * t + 1) * LANES : (2 * t + 2) * LANES] = sine
        left[ANG:, (2 * t) * LANES : (2 * t + 1) * LANES] = -sine
        left[ANG:, (2 * t + 1) * LANES : (2 * t + 2) * LANES] = cosine

    angle_rows = lax.broadcasted_iota(jnp.int32, (ANG, ANG), 0)
    sector = sub * 0
    for l in range(MERGES):
        bit = half_bits[l]
        for which in range(2):
            half = bit if which == 0 else 1 - bit
            at = pl.ds(pl.multiple_of(bit * ANG, ANG), ANG)
            taps = taps_ref[l, half, :, at]
            weights = weights_ref[l, half, :, at]
            total = jnp.zeros((ANG, ANG), f32)
            for t in range(TAPS):
                total = total + jnp.where(taps[t : t + 1, :] == angle_rows, weights[t : t + 1, :], 0.0)
            mats[l, which] = total.T.astype(bf16)
            offset = offsets_ref[l, sub] if which == 0 else offsets_ref[l, partners[l]]
            anchor = sector * (2 * ANG) + bit * ANG

            def fill(block, carry, l=l, which=which, offset=offset, anchor=anchor):
                start = pl.multiple_of(block * 32, 32)
                at = pl.ds(start, 32)
                row = lax.broadcasted_iota(jnp.int32, (32, LANES), 0)
                col = lax.broadcasted_iota(jnp.int32, (32, LANES), 1)
                column = 512 * rng + 32 * (col & 15) + 4 * (((col >> 4) - rng) & 7) + 1
                slope = (offset * (anchor + start + row)) & (PERIOD - 1)
                er, ei = unit_circle((slope * column) & (PERIOD - 1))
                tr, ti = unit_circle(slope)
                er, ei = er * 0.7071067811865476, ei * 0.7071067811865476
                for i in range(CHUNKS):
                    phase[l, which, i, 0, at] = er
                    phase[l, which, i, 1, at] = ei
                    if i < CHUNKS - 1:
                        er, ei = er * tr - ei * ti, er * ti + ei * tr
                return carry

            lax.fori_loop(0, ANG // 32, fill, 0)
        sector = sector * 2 + bit

    for i in range(CHUNKS):
        row = lax.broadcasted_iota(jnp.int32, (640, LANES), 0)
        col = lax.broadcasted_iota(jnp.int32, (640, LANES), 1)
        wanted = (64 * (row & 7) + (row >> 3) - 8) & 511
        place = 32 * (col & 15) + 4 * (((col >> 4) - rng) & 7) + i
        perm[:, i * LANES : (i + 1) * LANES] = jnp.where(place == wanted, 1.0, 0.0).astype(bf16)

    x_copies = {}
    m_copies = {}

    def contribution(l, which, i, ref):
        both = jnp.concatenate([ref[0], ref[1]], axis=1)
        proj = jnp.dot(mats[l, which], both, preferred_element_type=f32)
        pr, pi = proj[:, :LANES], proj[:, LANES:]
        er, ei = phase[l, which, i, 0], phase[l, which, i, 1]
        return pr * er - pi * ei, pr * ei + pi * er

    def pass_on(l, i):
        copy = pltpu.make_async_remote_copy(
            src_ref=image.at[l, i],
            dst_ref=image_in.at[l, i],
            send_sem=send_m.at[l, i],
            recv_sem=recv_m.at[l, i],
            device_id={"sub": partners[l]},
            device_id_type=MESH,
        )
        copy.start()
        m_copies[l, i] = copy
        re, im = contribution(l, 0, i, image.at[l, i])
        own_part[l, i, 0] = re
        own_part[l, i, 1] = im

    def step(kind, i):
        if kind == "beam":
            for j in (1, 2, 3):
                a_copies[i, j].wait_recv()
            own_copies[i].wait()
            total = jnp.dot(left[...], got[i].reshape(1024, 2 * LANES), preferred_element_type=f32)
            low, high = total[:, :LANES], total[:, LANES:]
            is_low = x_lo == 0
            part_out[i] = jnp.where(is_low, high, low).astype(bf16)
            copy = pltpu.make_async_remote_copy(
                src_ref=part_out.at[i],
                dst_ref=part_in.at[i],
                send_sem=send_x.at[i],
                recv_sem=recv_x.at[i],
                device_id={"rng": x_partner},
                device_id_type=MESH,
            )
            copy.start()
            x_copies[i] = copy
            part_own[i] = jnp.where(is_low, low, high)
        elif kind == "lead":
            x_copies[i].wait_recv()
            total = (part_own[i] + part_in[i].astype(f32)).astype(bf16)
            image[0, i, 0] = total[:ANG]
            image[0, i, 1] = total[ANG:]
            pass_on(0, i)
        else:
            l = int(kind[1])
            m_copies[l, i].wait_recv()
            re, im = contribution(l, 1, i, image_in.at[l, i])
            re = (re + own_part[l, i, 0]).astype(bf16)
            im = (im + own_part[l, i, 1]).astype(bf16)
            if l < MERGES - 1:
                image[l + 1, i, 0] = re
                image[l + 1, i, 1] = im
                pass_on(l + 1, i)
            else:
                final[0, :, i * LANES : (i + 1) * LANES] = re
                final[1, :, i * LANES : (i + 1) * LANES] = im

    for kind, i in order_of_steps():
        step(kind, i)

    def magnitude(at):
        re = lax.dot_general(perm[at], final[0], (((1,), (1,)), ((), ())), preferred_element_type=f32)
        im = lax.dot_general(perm[at], final[1], (((1,), (1,)), ((), ())), preferred_element_type=f32)
        return jnp.sqrt(re * re + im * im)

    halo_copies = []
    for side in range(2):
        at = slice(0, 64) if side else slice(576, 640)
        slab = magnitude(at)
        level[at] = slab
        halo_out[side] = slab.astype(bf16)
        copy = pltpu.make_async_remote_copy(
            src_ref=halo_out.at[side],
            dst_ref=halo_in.at[side],
            send_sem=send_h.at[side],
            recv_sem=recv_h.at[side],
            device_id={"rng": halo_partners[side]},
            device_id_type=MESH,
        )
        copy.start()
        halo_copies.append(copy)
    level[64:576] = magnitude(slice(64, 576))
    for copy in halo_copies:
        copy.wait_recv()

    place = lax.broadcasted_iota(jnp.int32, (8, 8, LANES), 1)

    def backward(v):
        return jnp.concatenate([v[7 - j : 8 - j] for j in range(8)], axis=0)

    def spread(h, carry):
        at = pl.ds(pl.multiple_of(h * LANES, LANES), LANES)
        u = level[:, at].reshape(80, 8, LANES)
        above = halo_in[0, :, at].astype(f32).reshape(8, 8, LANES)
        below = halo_in[1, :, at].astype(f32).reshape(8, 8, LANES)
        below = jnp.where(rng == 0, backward(u[8:16]), below)
        above = jnp.where(rng == 7, backward(u[64:72]), above)
        u = jnp.concatenate(
            [jnp.where(place == 0, below, u[:8]), u[8:72], jnp.where(place == 7, above, u[72:])], axis=0
        )
        for sweep in range(SWEEPS):
            diff = u[1:] - u[:-1]
            flux = diff / (2.0 + 0.5 * (diff * diff))
            u = u[1:-1] + (flux[1:] - flux[:-1])
        smooth[h] = u.reshape(512, LANES)
        return carry

    lax.fori_loop(0, 2, spread, 0)
    for h in range(2):
        for pair in range(4):
            both = [smooth[h, pl.ds(2 * pair + t, 64, stride=8), :] for t in range(2)]
            out_ref[h * LANES : (h + 1) * LANES, pair * LANES : (pair + 1) * LANES] = jnp.concatenate(both, axis=0).T

    for copy in list(a_copies.values()) + list(x_copies.values()) + list(m_copies.values()) + halo_copies:
        copy.wait_send()


def per_device(raw_echoes, merge_taps, merge_weights, track_offsets):
    second, twiddle, beam = make_tables()
    vmem = pl.BlockSpec(memory_space=pltpu.VMEM)
    smem = pl.BlockSpec(memory_space=pltpu.SMEM)
    anywhere = pl.BlockSpec(memory_space=pl.ANY)
    dma = pltpu.SemaphoreType.DMA
    return pl.pallas_call(
        kernel,
        out_shape=jax.ShapeDtypeStruct((ANG, 512), f32),
        in_specs=[anywhere, anywhere, anywhere, vmem, vmem, vmem, smem],
        out_specs=vmem,
        scratch_shapes=[
            pltpu.VMEM((2, 128, 4096), bf16),
            pltpu.VMEM((GROUPS, 256, 256), bf16),
            pltpu.VMEM((2, ANG, 4, LANES), bf16),
            pltpu.VMEM((2 * ANG, 1024), bf16),
            pltpu.VMEM((GROUPS, 128, 256), bf16),
            pltpu.VMEM((GROUPS, 128, 256), f32),
            pltpu.VMEM((CHUNKS, 4, 2, 128, 2 * LANES), bf16),
            pltpu.VMEM((CHUNKS, 4, 2, 128, 2 * LANES), bf16),
            pltpu.VMEM((CHUNKS, 2 * ANG, LANES), bf16),
            pltpu.VMEM((CHUNKS, 2 * ANG, LANES), bf16),
            pltpu.VMEM((CHUNKS, 2 * ANG, LANES), f32),
            pltpu.VMEM((MERGES, CHUNKS, 2, ANG, LANES), bf16),
            pltpu.VMEM((MERGES, CHUNKS, 2, ANG, LANES), bf16),
            pltpu.VMEM((MERGES, CHUNKS, 2, ANG, LANES), f32),
            pltpu.VMEM((MERGES, 2, CHUNKS, 2, ANG, LANES), f32),
            pltpu.VMEM((MERGES, 2, ANG, ANG), bf16),
            pltpu.VMEM((640, 512), bf16),
            pltpu.VMEM((2, ANG, 512), bf16),
            pltpu.VMEM((640, ANG), f32),
            pltpu.VMEM((2, 512, LANES), f32),
            pltpu.VMEM((2, 64, ANG), bf16),
            pltpu.VMEM((2, 64, ANG), bf16),
            dma((4,)),
            dma((CHUNKS,)),
            dma((CHUNKS, 3)),
            dma((CHUNKS, 3)),
            dma((CHUNKS,)),
            dma((CHUNKS,)),
            dma((MERGES, CHUNKS)),
            dma((MERGES, CHUNKS)),
            dma((2,)),
            dma((2,)),
        ],
        compiler_params=pltpu.CompilerParams(
            collective_id=0, has_side_effects=True, vmem_limit_bytes=56 << 20
        ),
        name="backproject",
    )(
        raw_echoes,
        jnp.asarray(second),
        jnp.asarray(beam),
        jnp.asarray(twiddle),
        merge_taps,
        merge_weights,
        track_offsets,
    )


def solution(mesh):
    in_specs = (P(None, ("sub", "rng"), None), P(), P(), P())
    out_specs = P("sub", "rng")
    return jax.shard_map(
        per_device, mesh=mesh, in_specs=in_specs, out_specs=out_specs, check_vma=False
    )
```

```python
import functools
import math

import jax
import jax.numpy as jnp
import numpy as np
from jax import lax
from jax.experimental import pallas as pl
from jax.experimental.pallas import tpu as pltpu
from jax.sharding import PartitionSpec as P

FACTOR = 64
ANG = 256
TAPS = 8
MERGES = 4
SWEEPS = 8
PERIOD = 8192
LANES = 128
CHUNKS = 8
ORDER = (0, 4, 1, 5, 2, 6, 3, 7)
GROUPS = 8
MESH = pl.DeviceIdType.MESH

bf16 = jnp.bfloat16
f32 = jnp.float32


def make_tables():
    tile = np.arange(LANES)
    b = np.arange(LANES)
    second = np.zeros((4, 2, LANES, 2, LANES))
    real = tile // 64 == 0
    for g in range(4):
        for half in range(2):
            r = 4 * half + (tile // 16 - g) % 4
            d = 16 * r + tile % 16
            angle = 2.0 * np.pi / 128.0 * ((b[:, None] * d[None, :]) % 128)
            cosine, sine = np.cos(angle) / FACTOR, np.sin(angle) / FACTOR
            second[g, 0, :, half] = np.where(real, cosine, -sine)
            second[g, 1, :, half] = np.where(real, sine, cosine)
    second = second.reshape(4, 2 * LANES, 2 * LANES)
    c = np.arange(32)
    angle = 2.0 * np.pi / 4096.0 * (c[:, None] * b[None, :])
    twiddle = np.stack([np.cos(angle), np.sin(angle)])
    a = np.arange(ANG) - ANG // 2
    q = np.arange(1024)
    angle = 2.0 * np.pi / 1024.0 * ((a[:, None] * q[None, :]) % 1024)
    beam = np.stack([np.cos(angle), np.sin(angle)]) / 32.0
    beam = beam.reshape(2, ANG, 4, 2, LANES).transpose(3, 0, 1, 2, 4).reshape(2, 2 * ANG, 512)
    return (
        second.astype(jnp.bfloat16),
        twiddle.astype(np.float32),
        np.ascontiguousarray(beam).astype(jnp.bfloat16),
    )


def transform_eight(z):
    half = math.sqrt(0.5)

    def four(v):
        (ar, ai), (br, bi), (cr, ci), (dr, di) = v
        sr, si, tr, ti = ar + cr, ai + ci, ar - cr, ai - ci
        ur, ui, vr, vi = br + dr, bi + di, br - dr, bi - di
        return [(sr + ur, si + ui), (tr + vi, ti - vr), (sr - ur, si - ui), (tr - vi, ti + vr)]

    even = four(z[0::2])
    odd = four(z[1::2])
    (o0r, o0i), (o1r, o1i), (o2r, o2i), (o3r, o3i) = odd
    turned = [
        (o0r, o0i),
        ((o1r + o1i) * half, (o1i - o1r) * half),
        (o2i, -o2r),
        ((o3i - o3r) * half, (-o3i - o3r) * half),
    ]
    low = [(er + tr, ei + ti) for (er, ei), (tr, ti) in zip(even, turned)]
    high = [(er - tr, ei - ti) for (er, ei), (tr, ti) in zip(even, turned)]
    return low + high


def unit_circle(steps):
    moved = steps + 1024
    quadrant = moved >> 11
    x = ((moved & 2047) - 1024).astype(f32) * (2.0 * math.pi / PERIOD)
    z = x * x
    sine = x * (1.0 + z * (-1.0 / 6.0 + z * (1.0 / 120.0 - z * (1.0 / 5040.0))))
    cosine = 1.0 + z * (-0.5 + z * (1.0 / 24.0 + z * (-1.0 / 720.0 + z * (1.0 / 40320.0))))
    swap = (quadrant & 1) == 1
    out_cos = jnp.where(swap, sine, cosine)
    out_sin = jnp.where(swap, cosine, sine)
    out_cos = jnp.where(((quadrant + 1) & 2) == 2, -out_cos, out_cos)
    out_sin = jnp.where((quadrant & 2) == 2, -out_sin, out_sin)
    return out_cos, out_sin


def order_of_steps():
    return [
        ("beam", 0), ("tab", 3), ("beam", 4), ("tab", 0), ("beam", 1), ("lead", 0), ("tab", 1),
        ("tab", 2), ("m0", 0), ("beam", 5), ("lead", 1), ("lead", 4), ("m0", 1), ("m0", 4),
        ("m1", 0), ("beam", 2), ("lead", 5), ("beam", 6), ("m1", 1), ("m2", 0), ("m0", 5),
        ("m1", 4), ("lead", 2), ("m2", 1), ("m0", 2), ("lead", 6), ("beam", 7), ("m1", 5),
        ("m0", 6), ("m2", 4), ("beam", 3), ("m1", 2), ("lead", 7), ("m2", 5), ("m0", 7),
        ("m1", 6), ("lead", 3), ("m2", 2), ("m3", 0), ("m0", 3), ("m1", 7), ("m2", 6),
        ("m1", 3), ("m2", 7), ("perm", 0), ("m2", 3), ("m3", 5), ("m3", 6), ("m3", 2),
        ("m3", 7), ("m3", 1), ("m3", 4), ("m3", 3),
    ]


def kernel(
    raw_hbm, second_hbm, beam_hbm, twiddle_ref, taps_ref, weights_ref, offsets_ref, out_ref,
    raw, second, beam, rows_buf, wide, sent, got, part_out, part_in, part_own,
    image, image_in, phase, mats, perm, final, level, smooth, halo_out, halo_in,
    in_sem, own_sem, send_a, recv_a, send_x, recv_x, send_m, recv_m, send_h, recv_h,
):
    sub = lax.axis_index("sub")
    rng = lax.axis_index("rng")
    x_lo = rng % 2
    y = rng // 2

    half_bits = [(sub // 2**l) % 2 for l in range(MERGES)]
    partners = [sub + 2**l - 2 * 2**l * half_bits[l] for l in range(MERGES)]
    x_partner = rng + 1 - 2 * x_lo
    y_partners = [((y + j) % 4) * 2 + x_lo for j in (1, 2, 3)]
    halo_partners = [(rng + 7) % 8, (rng + 1) % 8]

    raw_copies = [
        pltpu.make_async_copy(raw_hbm.at[:, pl.ds(64 * h, 64)], raw.at[:, pl.ds(64 * h, 64)], in_sem.at[h])
        for h in range(2)
    ]
    second_copy = pltpu.make_async_copy(second_hbm, second, in_sem.at[2])
    beam_copy = pltpu.make_async_copy(beam_hbm.at[x_lo], beam, in_sem.at[3])
    for copy in raw_copies:
        copy.start()
    second_copy.start()
    beam_copy.start()

    barrier = pltpu.get_barrier_semaphore()
    ids = [{"rng": t} for t in y_partners + [x_partner] + halo_partners] + [{"sub": t} for t in partners]
    for one in ids:
        pl.semaphore_signal(barrier, inc=1, device_id=one, device_id_type=MESH)

    lane = lax.broadcasted_iota(jnp.int32, (16, LANES), 1)
    group_bits = [((lane // 16) // 2**t) % 2 == 1 for t in range(2)]
    a_copies = {}
    own_copies = {}

    def transform(i, first):
        def rows(block, carry):
            at = pl.ds(pl.multiple_of(block * 16, 16), 16)

            def load(part, a):
                return raw[part, at, a * LANES : (a + 1) * LANES].astype(f32)

            mixed = []
            for m in range(8):
                v = [(load(0, m + 8 * j), load(1, m + 8 * j)) for j in range(4)]
                if i % 2 == 0:
                    sr, si = v[0][0] + v[2][0], v[0][1] + v[2][1]
                    tr, ti = v[1][0] + v[3][0], v[1][1] + v[3][1]
                    zr, zi = (sr + tr, si + ti) if i == 0 else (sr - tr, si - ti)
                else:
                    sr, si = v[0][0] - v[2][0], v[0][1] - v[2][1]
                    tr, ti = v[1][0] - v[3][0], v[1][1] - v[3][1]
                    zr, zi = (sr + ti, si - tr) if i == 1 else (sr - ti, si + tr)
                if i * m:
                    turn = 2.0 * math.pi * i * m / 32.0
                    wc, ws = math.cos(turn), math.sin(turn)
                    zr, zi = zr * wc + zi * ws, zi * wc - zr * ws
                mixed.append((zr, zi))
            for g, (zr, zi) in enumerate(transform_eight(mixed)):
                c = i + 4 * g
                wc = twiddle_ref[0, c : c + 1, :]
                ws = twiddle_ref[1, c : c + 1, :]
                rows_buf[g, at, 0:LANES] = (zr * wc + zi * ws).astype(bf16)
                rows_buf[g, at, LANES : 2 * LANES] = (zi * wc - zr * ws).astype(bf16)
            return carry

        if first:
            raw_copies[0].wait()
            lax.fori_loop(0, 4, rows, 0)
            raw_copies[1].wait()
            lax.fori_loop(4, 8, rows, 0)
            second_copy.wait()
        else:
            lax.fori_loop(0, 8, rows, 0)
        for odd in range(2):
            for g in range(4):
                wide[g] = jnp.dot(rows_buf[2 * g + odd], second[g], preferred_element_type=f32)
            share(i + 4 * odd, first and odd == 0)

    def share(i, first):
        def pick(block, carry):
            at = pl.ds(pl.multiple_of(block * 16, 16), 16)
            for part in range(2):
                tiles = [wide[(4 - r) % 4, at, part * LANES : (part + 1) * LANES] for r in range(4)]
                for t in range(2):
                    tiles = [jnp.where(group_bits[t], tiles[(r - 2**t) % 4], tiles[r]) for r in range(4)]
                for r in range(4):
                    sent[i, 2 * part + r // 2, at, (r % 2) * LANES : (r % 2 + 1) * LANES] = tiles[r].astype(bf16)
            return carry

        lax.fori_loop(0, 8, pick, 0)
        if first:
            pl.semaphore_wait(barrier, len(ids))
        for j in (2, 1, 3):
            target = (y + j) % 4
            copy = pltpu.make_async_remote_copy(
                src_ref=sent.at[i, target],
                dst_ref=got.at[i, y],
                send_sem=send_a.at[i, j - 1],
                recv_sem=recv_a.at[i, j - 1],
                device_id={"rng": target * 2 + x_lo},
                device_id_type=MESH,
            )
            copy.start()
            a_copies[i, j] = copy
        own_copies[i] = pltpu.make_async_copy(sent.at[i, y], got.at[i, y], own_sem.at[i])
        own_copies[i].start()

    for i in range(4):
        transform(i, i == 0)

    angle_rows = lax.broadcasted_iota(jnp.int32, (ANG, ANG), 0)
    sectors = [sub * 0]
    for l in range(MERGES - 1):
        sectors.append(sectors[l] * 2 + half_bits[l])

    def tables(l):
        bit = half_bits[l]
        for which in range(2):
            half = bit if which == 0 else 1 - bit
            at = pl.ds(pl.multiple_of(bit * ANG, ANG), ANG)
            taps = taps_ref[l, half, :, at]
            weights = weights_ref[l, half, :, at]
            total = jnp.zeros((ANG, ANG), f32)
            for t in range(TAPS):
                total = total + jnp.where(taps[t : t + 1, :] == angle_rows, weights[t : t + 1, :], 0.0)
            mats[l, which] = total.T.astype(bf16)
            offset = offsets_ref[l, sub] if which == 0 else offsets_ref[l, partners[l]]
            anchor = sectors[l] * (2 * ANG) + bit * ANG

            def fill(block, carry, which=which, offset=offset, anchor=anchor):
                start = pl.multiple_of(block * 32, 32)
                at = pl.ds(start, 32)
                row = lax.broadcasted_iota(jnp.int32, (32, LANES), 0)
                col = lax.broadcasted_iota(jnp.int32, (32, LANES), 1)
                column = 512 * rng + 32 * (col & 15) + 8 * (((col >> 4) - rng) & 3) + 1
                slope = (offset * (anchor + start + row)) & (PERIOD - 1)
                er, ei = unit_circle((slope * column) & (PERIOD - 1))
                tr, ti = unit_circle(slope)
                er, ei = er * 0.7071067811865476, ei * 0.7071067811865476
                ei = jnp.where(col < 64, -ei, ei)
                ti = jnp.where(col < 64, -ti, ti)
                for i in range(CHUNKS):
                    phase[l, which, i, 0, at] = er
                    phase[l, which, i, 1, at] = ei
                    if i < CHUNKS - 1:
                        er, ei = er * tr - ei * ti, er * ti + ei * tr
                return carry

            lax.fori_loop(0, ANG // 32, fill, 0)

    def orders():
        for i in range(CHUNKS):
            row = lax.broadcasted_iota(jnp.int32, (640, LANES), 0)
            col = lax.broadcasted_iota(jnp.int32, (640, LANES), 1)
            wanted = (64 * (row & 7) + (row >> 3) - 8) & 511
            place = 32 * (col & 15) + 8 * (((col >> 4) - rng) & 3) + i
            for part in range(2):
                here = (place == wanted) & ((col >> 6) == part)
                perm[part, :, i * LANES : (i + 1) * LANES] = jnp.where(here, 1.0, 0.0).astype(bf16)

    x_copies = {}
    m_copies = {}

    def contribution(l, which, i, ref):
        proj = jnp.dot(mats[l, which], ref[...], preferred_element_type=f32)
        return proj * phase[l, which, i, 0] + pltpu.roll(proj, 64, 1) * phase[l, which, i, 1]

    def pass_on(l, i):
        copy = pltpu.make_async_remote_copy(
            src_ref=image.at[l, i],
            dst_ref=image_in.at[l, i],
            send_sem=send_m.at[l, i],
            recv_sem=recv_m.at[l, i],
            device_id={"sub": partners[l]},
            device_id_type=MESH,
        )
        copy.start()
        m_copies[l, i] = copy

    def step(kind, i):
        if kind == "tab":
            tables(i)
        elif kind == "perm":
            orders()
        elif kind == "beam":
            if i == ORDER[0]:
                beam_copy.wait()
            for j in (1, 2, 3):
                a_copies[i, j].wait_recv()
            own_copies[i].wait()
            total = jnp.dot(beam[...], got[i].reshape(512, 2 * LANES), preferred_element_type=f32)
            low, high = [
                total[:ANG, at] + turned * pltpu.roll(total[ANG:, at], 64, 1)
                for at in (slice(0, LANES), slice(LANES, 2 * LANES))
            ]
            is_low = x_lo == 0
            part_out[i] = jnp.where(is_low, high, low).astype(bf16)
            copy = pltpu.make_async_remote_copy(
                src_ref=part_out.at[i],
                dst_ref=part_in.at[i],
                send_sem=send_x.at[i],
                recv_sem=recv_x.at[i],
                device_id={"rng": x_partner},
                device_id_type=MESH,
            )
            copy.start()
            x_copies[i] = copy
            part_own[i] = jnp.where(is_low, low, high)
        elif kind == "lead":
            x_copies[i].wait_recv()
            image[0, i] = (part_own[i] + part_in[i].astype(f32)).astype(bf16)
            pass_on(0, i)
        else:
            l = int(kind[1])
            m_copies[l, i].wait_recv()
            merged = (contribution(l, 0, i, image.at[l, i]) + contribution(l, 1, i, image_in.at[l, i])).astype(bf16)
            if l < MERGES - 1:
                image[l + 1, i] = merged
                pass_on(l + 1, i)
            else:
                final[:, i * LANES : (i + 1) * LANES] = merged

    turned = jnp.where(lax.broadcasted_iota(jnp.int32, (ANG, LANES), 1) < 64, 1.0, -1.0)
    for kind, i in order_of_steps():
        step(kind, i)

    def magnitude(at):
        re = lax.dot_general(perm[0, at], final[...], (((1,), (1,)), ((), ())), preferred_element_type=f32)
        im = lax.dot_general(perm[1, at], final[...], (((1,), (1,)), ((), ())), preferred_element_type=f32)
        return jnp.sqrt(re * re + im * im)

    halo_copies = []
    for side in range(2):
        at = slice(0, 64) if side else slice(576, 640)
        slab = magnitude(at)
        level[at] = slab
        halo_out[side] = slab.astype(bf16)
        copy = pltpu.make_async_remote_copy(
            src_ref=halo_out.at[side],
            dst_ref=halo_in.at[side],
            send_sem=send_h.at[side],
            recv_sem=recv_h.at[side],
            device_id={"rng": halo_partners[side]},
            device_id_type=MESH,
        )
        copy.start()
        halo_copies.append(copy)
    level[64:576] = magnitude(slice(64, 576))
    for copy in halo_copies:
        copy.wait_recv()

    place = lax.broadcasted_iota(jnp.int32, (8, 8, LANES), 1)

    def backward(v):
        return jnp.concatenate([v[7 - j : 8 - j] for j in range(8)], axis=0)

    def spread(h, carry):
        at = pl.ds(pl.multiple_of(h * LANES, LANES), LANES)
        u = level[:, at].reshape(80, 8, LANES)
        above = halo_in[0, :, at].astype(f32).reshape(8, 8, LANES)
        below = halo_in[1, :, at].astype(f32).reshape(8, 8, LANES)
        below = jnp.where(rng == 0, backward(u[8:16]), below)
        above = jnp.where(rng == 7, backward(u[64:72]), above)
        u = jnp.concatenate(
            [jnp.where(place == 0, below, u[:8]), u[8:72], jnp.where(place == 7, above, u[72:])], axis=0
        )
        for sweep in range(SWEEPS):
            diff = u[1:] - u[:-1]
            flux = diff / (2.0 + 0.5 * (diff * diff))
            u = u[1:-1] + (flux[1:] - flux[:-1])
        smooth[h] = u.reshape(512, LANES)
        return carry

    lax.fori_loop(0, 2, spread, 0)
    for h in range(2):
        for pair in range(4):
            both = [smooth[h, pl.ds(2 * pair + t, 64, stride=8), :] for t in range(2)]
            out_ref[h * LANES : (h + 1) * LANES, pair * LANES : (pair + 1) * LANES] = jnp.concatenate(both, axis=0).T

    for copy in list(a_copies.values()) + list(x_copies.values()) + list(m_copies.values()) + halo_copies:
        copy.wait_send()


def per_device(raw_echoes, merge_taps, merge_weights, track_offsets):
    second, twiddle, beam = make_tables()
    vmem = pl.BlockSpec(memory_space=pltpu.VMEM)
    smem = pl.BlockSpec(memory_space=pltpu.SMEM)
    anywhere = pl.BlockSpec(memory_space=pl.ANY)
    dma = pltpu.SemaphoreType.DMA
    return pl.pallas_call(
        kernel,
        out_shape=jax.ShapeDtypeStruct((ANG, 512), f32),
        in_specs=[anywhere, anywhere, anywhere, vmem, vmem, vmem, smem],
        out_specs=vmem,
        scratch_shapes=[
            pltpu.VMEM((2, 128, 4096), bf16),
            pltpu.VMEM((4, 256, 256), bf16),
            pltpu.VMEM((2 * ANG, 512), bf16),
            pltpu.VMEM((GROUPS, 128, 256), bf16),
            pltpu.VMEM((4, 128, 256), f32),
            pltpu.VMEM((CHUNKS, 4, 128, 2 * LANES), bf16),
            pltpu.VMEM((CHUNKS, 4, 128, 2 * LANES), bf16),
            pltpu.VMEM((CHUNKS, ANG, LANES), bf16),
            pltpu.VMEM((CHUNKS, ANG, LANES), bf16),
            pltpu.VMEM((CHUNKS, ANG, LANES), f32),
            pltpu.VMEM((MERGES, CHUNKS, ANG, LANES), bf16),
            pltpu.VMEM((MERGES, CHUNKS, ANG, LANES), bf16),
            pltpu.VMEM((MERGES, 2, CHUNKS, 2, ANG, LANES), f32),
            pltpu.VMEM((MERGES, 2, ANG, ANG), bf16),
            pltpu.VMEM((2, 640, CHUNKS * LANES), bf16),
            pltpu.VMEM((ANG, CHUNKS * LANES), bf16),
            pltpu.VMEM((640, ANG), f32),
            pltpu.VMEM((2, 512, LANES), f32),
            pltpu.VMEM((2, 64, ANG), bf16),
            pltpu.VMEM((2, 64, ANG), bf16),
            dma((4,)),
            dma((CHUNKS,)),
            dma((CHUNKS, 3)),
            dma((CHUNKS, 3)),
            dma((CHUNKS,)),
            dma((CHUNKS,)),
            dma((MERGES, CHUNKS)),
            dma((MERGES, CHUNKS)),
            dma((2,)),
            dma((2,)),
        ],
        compiler_params=pltpu.CompilerParams(
            collective_id=0, has_side_effects=True, vmem_limit_bytes=56 << 20
        ),
        name="backproject",
    )(
        raw_echoes,
        jnp.asarray(second),
        jnp.asarray(beam),
        jnp.asarray(twiddle),
        merge_taps,
        merge_weights,
        track_offsets,
    )


def solution(mesh):
    in_specs = (P(None, ("sub", "rng"), None), P(), P(), P())
    out_specs = P("sub", "rng")
    return jax.shard_map(
        per_device, mesh=mesh, in_specs=in_specs, out_specs=out_specs, check_vma=False
    )
```

```python
import functools
import math

import jax
import jax.numpy as jnp
import numpy as np
from jax import lax
from jax.experimental import pallas as pl
from jax.experimental.pallas import tpu as pltpu
from jax.sharding import PartitionSpec as P

FACTOR = 64
ANG = 256
TAPS = 8
MERGES = 4
SWEEPS = 8
PERIOD = 8192
LANES = 128
CHUNKS = 8
UNITS = ((0,), (1,), (2,), (3,), (4,), (5,), (6,), (7,))
GROUPS = 8
MESH = pl.DeviceIdType.MESH

bf16 = jnp.bfloat16
f32 = jnp.float32


def make_tables():
    tile = np.arange(LANES)
    b = np.arange(LANES)
    second = np.zeros((4, 2, LANES, 2, LANES))
    real = tile // 64 == 0
    for g in range(4):
        for half in range(2):
            r = 4 * half + (tile // 16 - g) % 4
            d = 16 * r + tile % 16
            angle = 2.0 * np.pi / 128.0 * ((b[:, None] * d[None, :]) % 128)
            cosine, sine = np.cos(angle) / FACTOR, np.sin(angle) / FACTOR
            second[g, 0, :, half] = np.where(real, cosine, -sine)
            second[g, 1, :, half] = np.where(real, sine, cosine)
    second = second.reshape(4, 2 * LANES, 2 * LANES)
    c = np.arange(32)
    angle = 2.0 * np.pi / 4096.0 * (c[:, None] * b[None, :])
    twiddle = np.stack([np.cos(angle), np.sin(angle)])
    a = np.arange(ANG) - ANG // 2
    q = np.arange(1024)
    angle = 2.0 * np.pi / 1024.0 * ((a[:, None] * q[None, :]) % 1024)
    beam = np.stack([np.cos(angle), np.sin(angle)]) / 32.0
    beam = beam.reshape(2, ANG, 4, 2, LANES).transpose(3, 0, 1, 2, 4).reshape(2, 2 * ANG, 512)
    return (
        second.astype(jnp.bfloat16),
        twiddle.astype(np.float32),
        np.ascontiguousarray(beam).astype(jnp.bfloat16),
    )


def transform_eight(z):
    half = math.sqrt(0.5)

    def four(v):
        (ar, ai), (br, bi), (cr, ci), (dr, di) = v
        sr, si, tr, ti = ar + cr, ai + ci, ar - cr, ai - ci
        ur, ui, vr, vi = br + dr, bi + di, br - dr, bi - di
        return [(sr + ur, si + ui), (tr + vi, ti - vr), (sr - ur, si - ui), (tr - vi, ti + vr)]

    even = four(z[0::2])
    odd = four(z[1::2])
    (o0r, o0i), (o1r, o1i), (o2r, o2i), (o3r, o3i) = odd
    turned = [
        (o0r, o0i),
        ((o1r + o1i) * half, (o1i - o1r) * half),
        (o2i, -o2r),
        ((o3i - o3r) * half, (-o3i - o3r) * half),
    ]
    low = [(er + tr, ei + ti) for (er, ei), (tr, ti) in zip(even, turned)]
    high = [(er - tr, ei - ti) for (er, ei), (tr, ti) in zip(even, turned)]
    return low + high


def unit_circle(steps):
    moved = steps + 1024
    quadrant = moved >> 11
    x = ((moved & 2047) - 1024).astype(f32) * (2.0 * math.pi / PERIOD)
    z = x * x
    sine = x * (1.0 + z * (-1.0 / 6.0 + z * (1.0 / 120.0 - z * (1.0 / 5040.0))))
    cosine = 1.0 + z * (-0.5 + z * (1.0 / 24.0 + z * (-1.0 / 720.0 + z * (1.0 / 40320.0))))
    swap = (quadrant & 1) == 1
    out_cos = jnp.where(swap, sine, cosine)
    out_sin = jnp.where(swap, cosine, sine)
    out_cos = jnp.where(((quadrant + 1) & 2) == 2, -out_cos, out_cos)
    out_sin = jnp.where((quadrant & 2) == 2, -out_sin, out_sin)
    return out_cos, out_sin


def order_of_steps():
    return [
        ("dft", 0), ("dft", 1), ("dft", 2), ("beam", 0), ("dft", 3), ("tab", 0), ("beam", 1),
        ("lead", 0), ("tab", 2), ("beam", 2), ("m0", 0), ("tab", 1), ("lead", 1), ("beam", 3),
        ("m0", 1), ("lead", 2), ("beam", 4), ("m1", 0), ("lead", 3), ("m0", 2), ("beam", 5),
        ("m1", 1), ("m0", 3), ("m2", 0), ("lead", 4), ("beam", 6), ("m1", 2), ("m0", 4),
        ("m2", 1), ("lead", 5), ("beam", 7), ("m1", 3), ("m0", 5), ("m2", 2), ("lead", 6),
        ("tab", 3), ("m1", 4), ("m0", 6), ("m2", 3), ("lead", 7), ("m1", 5), ("m0", 7),
        ("m2", 4), ("m1", 6), ("m3", 1), ("m2", 5), ("perm", 0), ("m1", 7), ("m3", 0),
        ("m2", 6), ("m2", 7), ("m3", 5), ("m3", 2), ("m3", 3), ("m3", 6), ("m3", 4),
        ("m3", 7),
    ]


def kernel(
    raw_hbm, second_hbm, beam_hbm, twiddle_hbm, taps_hbm, weights_hbm, offsets_ref, out_ref,
    raw, second, beam, twiddle_ref, taps_ref, weights_ref, rows_buf, wide, sent, got, part_out, part_in, part_own,
    image, image_in, phase, mats, perm, final, level, halo_out, halo_in,
    in_sem, own_sem, send_a, recv_a, send_x, recv_x, send_m, recv_m, send_h, recv_h,
):
    sub = lax.axis_index("sub")
    rng = lax.axis_index("rng")
    x_lo = rng % 2
    y = rng // 2

    half_bits = [(sub // 2**l) % 2 for l in range(MERGES)]
    partners = [sub + 2**l - 2 * 2**l * half_bits[l] for l in range(MERGES)]
    x_partner = rng + 1 - 2 * x_lo
    y_partners = [((y + j) % 4) * 2 + x_lo for j in (1, 2, 3)]
    halo_partners = [(rng + 7) % 8, (rng + 1) % 8]

    raw_copies = [
        pltpu.make_async_copy(raw_hbm.at[:, pl.ds(64 * h, 64)], raw.at[:, pl.ds(64 * h, 64)], in_sem.at[h])
        for h in range(2)
    ]
    second_copy = pltpu.make_async_copy(second_hbm, second, in_sem.at[2])
    beam_copy = pltpu.make_async_copy(beam_hbm.at[x_lo], beam, in_sem.at[3])
    twiddle_copy = pltpu.make_async_copy(twiddle_hbm, twiddle_ref, in_sem.at[4])
    taps_copy = pltpu.make_async_copy(taps_hbm, taps_ref, in_sem.at[5])
    weights_copy = pltpu.make_async_copy(weights_hbm, weights_ref, in_sem.at[6])
    twiddle_copy.start()
    for copy in raw_copies:
        copy.start()
    second_copy.start()
    beam_copy.start()
    taps_copy.start()
    weights_copy.start()

    barrier = pltpu.get_barrier_semaphore()
    ids = [{"rng": t} for t in y_partners + [x_partner] + halo_partners] + [{"sub": t} for t in partners]
    for one in ids:
        pl.semaphore_signal(barrier, inc=1, device_id=one, device_id_type=MESH)

    lane = lax.broadcasted_iota(jnp.int32, (16, LANES), 1)
    group_bits = [((lane // 16) // 2**t) % 2 == 1 for t in range(2)]
    a_copies = {}
    own_copies = {}

    def transform(i, first):
        def rows(block, carry):
            at = pl.ds(pl.multiple_of(block * 16, 16), 16)

            def load(part, a):
                return raw[part, at, a * LANES : (a + 1) * LANES].astype(f32)

            mixed = []
            for m in range(8):
                v = [(load(0, m + 8 * j), load(1, m + 8 * j)) for j in range(4)]
                if i % 2 == 0:
                    sr, si = v[0][0] + v[2][0], v[0][1] + v[2][1]
                    tr, ti = v[1][0] + v[3][0], v[1][1] + v[3][1]
                    zr, zi = (sr + tr, si + ti) if i == 0 else (sr - tr, si - ti)
                else:
                    sr, si = v[0][0] - v[2][0], v[0][1] - v[2][1]
                    tr, ti = v[1][0] - v[3][0], v[1][1] - v[3][1]
                    zr, zi = (sr + ti, si - tr) if i == 1 else (sr - ti, si + tr)
                if i * m:
                    turn = 2.0 * math.pi * i * m / 32.0
                    wc, ws = math.cos(turn), math.sin(turn)
                    zr, zi = zr * wc + zi * ws, zi * wc - zr * ws
                mixed.append((zr, zi))
            for g, (zr, zi) in enumerate(transform_eight(mixed)):
                c = i + 4 * g
                wc = twiddle_ref[0, c : c + 1, :]
                ws = twiddle_ref[1, c : c + 1, :]
                rows_buf[g, at, 0:LANES] = (zr * wc + zi * ws).astype(bf16)
                rows_buf[g, at, LANES : 2 * LANES] = (zi * wc - zr * ws).astype(bf16)
            return carry

        if first:
            twiddle_copy.wait()
            raw_copies[0].wait()
            lax.fori_loop(0, 4, rows, 0)
            raw_copies[1].wait()
            lax.fori_loop(4, 8, rows, 0)
            second_copy.wait()
        else:
            lax.fori_loop(0, 8, rows, 0)
        for odd in range(2):
            for g in range(4):
                wide[g] = jnp.dot(rows_buf[2 * g + odd], second[g], preferred_element_type=f32)
            share(2 * i + odd, first and odd == 0)

    def share(i, first):
        def pick(block, carry):
            at = pl.ds(pl.multiple_of(block * 16, 16), 16)
            for part in range(2):
                tiles = [wide[(4 - r) % 4, at, part * LANES : (part + 1) * LANES] for r in range(4)]
                for t in range(2):
                    tiles = [jnp.where(group_bits[t], tiles[(r - 2**t) % 4], tiles[r]) for r in range(4)]
                for r in range(4):
                    sent[2 * part + r // 2, i, at, (r % 2) * LANES : (r % 2 + 1) * LANES] = tiles[r].astype(bf16)
            return carry

        lax.fori_loop(0, 8, pick, 0)
        if first:
            pl.semaphore_wait(barrier, len(ids))
        for n, unit in enumerate(UNITS):
            if unit[-1] == i:
                send_unit(n, pl.ds(unit[0], len(unit)))

    def send_unit(n, at):
        for j in (2, 1, 3):
            target = (y + j) % 4
            copy = pltpu.make_async_remote_copy(
                src_ref=sent.at[target, at],
                dst_ref=got.at[at, y],
                send_sem=send_a.at[n, j - 1],
                recv_sem=recv_a.at[n, j - 1],
                device_id={"rng": target * 2 + x_lo},
                device_id_type=MESH,
            )
            copy.start()
            a_copies[n, j] = copy
        own_copies[n] = pltpu.make_async_copy(sent.at[y, at], got.at[at, y], own_sem.at[n])
        own_copies[n].start()

    angle_rows = lax.broadcasted_iota(jnp.int32, (ANG, ANG), 0)
    sectors = [sub * 0]
    for l in range(MERGES - 1):
        sectors.append(sectors[l] * 2 + half_bits[l])

    def tables(l):
        if l == 0:
            taps_copy.wait()
            weights_copy.wait()
        bit = half_bits[l]
        for which in range(2):
            half = bit if which == 0 else 1 - bit
            at = pl.ds(pl.multiple_of(bit * ANG, ANG), ANG)
            taps = taps_ref[l, half, :, at]
            weights = weights_ref[l, half, :, at]
            total = jnp.zeros((ANG, ANG), f32)
            for t in range(TAPS):
                total = total + jnp.where(taps[t : t + 1, :] == angle_rows, weights[t : t + 1, :], 0.0)
            mats[l, which] = total.T.astype(bf16)
            offset = offsets_ref[l, sub] if which == 0 else offsets_ref[l, partners[l]]
            anchor = sectors[l] * (2 * ANG) + bit * ANG

            def fill(block, carry, which=which, offset=offset, anchor=anchor):
                start = pl.multiple_of(block * 32, 32)
                at = pl.ds(start, 32)
                row = lax.broadcasted_iota(jnp.int32, (32, LANES), 0)
                col = lax.broadcasted_iota(jnp.int32, (32, LANES), 1)
                column = 512 * rng + 32 * (col & 15) + 8 * (((col >> 4) - rng) & 3) + 1
                slope = (offset * (anchor + start + row)) & (PERIOD - 1)
                er, ei = unit_circle((slope * column) & (PERIOD - 1))
                tr, ti = unit_circle(slope)
                er, ei = er * 0.7071067811865476, ei * 0.7071067811865476
                ei = jnp.where(col < 64, -ei, ei)
                ti = jnp.where(col < 64, -ti, ti)
                for i in range(CHUNKS):
                    phase[l, which, 2 * (i % 4) + i // 4, 0, at] = er
                    phase[l, which, 2 * (i % 4) + i // 4, 1, at] = ei
                    if i < CHUNKS - 1:
                        er, ei = er * tr - ei * ti, er * ti + ei * tr
                return carry

            lax.fori_loop(0, ANG // 32, fill, 0)

    def orders():
        for i in range(4):
            row = lax.broadcasted_iota(jnp.int32, (640, LANES), 0)
            col = lax.broadcasted_iota(jnp.int32, (640, LANES), 1)
            wanted = (64 * (row & 7) + (row >> 3) - 8) & 511
            place = 32 * (col & 15) + 8 * (((col >> 4) - rng) & 3) + i
            late = 4 * (col >> 6)
            for part in range(2):
                here = place + (late if part == 0 else 4 - late) == wanted
                perm[part, :, i * LANES : (i + 1) * LANES] = jnp.where(here, 1.0, 0.0).astype(bf16)

    x_copies = {}
    m_copies = {}

    def contribution(l, which, unit, ref):
        proj = jnp.dot(
            mats[l, which],
            jnp.concatenate([ref[l, q] for q in unit], axis=1),
            preferred_element_type=f32,
        )
        parts = [proj[:, t * LANES : (t + 1) * LANES] for t in range(len(unit))]
        return [
            part * phase[l, which, q, 0] + pltpu.roll(part, 64, 1) * phase[l, which, q, 1]
            for part, q in zip(parts, unit)
        ]

    def pass_on(l, n):
        at = pl.ds(UNITS[n][0], len(UNITS[n]))
        copy = pltpu.make_async_remote_copy(
            src_ref=image.at[l, at],
            dst_ref=image_in.at[l, at],
            send_sem=send_m.at[l, n],
            recv_sem=recv_m.at[l, n],
            device_id={"sub": partners[l]},
            device_id_type=MESH,
        )
        copy.start()
        m_copies[l, n] = copy

    def step(kind, n):
        if kind == "dft":
            transform(n, n == 0)
            return
        if kind == "tab":
            tables(n)
            return
        if kind == "perm":
            orders()
            return
        unit = UNITS[n]
        if kind == "beam":
            if n == 0:
                beam_copy.wait()
            for j in (1, 2, 3):
                a_copies[n, j].wait_recv()
            own_copies[n].wait()
            both = jnp.concatenate([got[q].reshape(512, 2 * LANES) for q in unit], axis=1)
            total = jnp.dot(beam[...], both, preferred_element_type=f32)
            is_low = x_lo == 0
            owned = []
            for t, q in enumerate(unit):
                low, high = [
                    total[:ANG, at] + turned * pltpu.roll(total[ANG:, at], 64, 1)
                    for at in (slice(2 * t * LANES, (2 * t + 1) * LANES), slice((2 * t + 1) * LANES, (2 * t + 2) * LANES))
                ]
                part_out[q] = jnp.where(is_low, high, low).astype(bf16)
                owned.append(jnp.where(is_low, low, high))
            at = pl.ds(unit[0], len(unit))
            copy = pltpu.make_async_remote_copy(
                src_ref=part_out.at[at],
                dst_ref=part_in.at[at],
                send_sem=send_x.at[n],
                recv_sem=recv_x.at[n],
                device_id={"rng": x_partner},
                device_id_type=MESH,
            )
            copy.start()
            x_copies[n] = copy
            for q, value in zip(unit, owned):
                part_own[q] = value
        elif kind == "lead":
            x_copies[n].wait_recv()
            for q in unit:
                image[0, q] = (part_own[q] + part_in[q].astype(f32)).astype(bf16)
            pass_on(0, n)
        else:
            l = int(kind[1])
            m_copies[l, n].wait_recv()
            mine = contribution(l, 0, unit, image)
            theirs = contribution(l, 1, unit, image_in)
            for q, a, b in zip(unit, mine, theirs):
                merged = a + b
                if l < MERGES - 1:
                    image[l + 1, q] = merged.astype(bf16)
                    continue
                tile = (q // 2) * LANES
                if q % 2 == 0:
                    final[0, :, tile : tile + 64] = merged[:, :64].astype(bf16)
                    final[1, :, tile + 64 : tile + LANES] = merged[:, 64:].astype(bf16)
                else:
                    turn = pltpu.roll(merged, 64, 1)
                    final[1, :, tile : tile + 64] = turn[:, :64].astype(bf16)
                    final[0, :, tile + 64 : tile + LANES] = turn[:, 64:].astype(bf16)
            if l < MERGES - 1:
                pass_on(l + 1, n)

    turned = jnp.where(lax.broadcasted_iota(jnp.int32, (ANG, LANES), 1) < 64, 1.0, -1.0)
    for kind, i in order_of_steps():
        step(kind, i)

    def magnitude(at):
        re = lax.dot_general(perm[0, at], final[0], (((1,), (1,)), ((), ())), preferred_element_type=f32)
        im = lax.dot_general(perm[1, at], final[1], (((1,), (1,)), ((), ())), preferred_element_type=f32)
        return jnp.sqrt(re * re + im * im)

    halo_copies = []
    for side in range(2):
        at = slice(0, 64) if side else slice(576, 640)
        slab = magnitude(at)
        level[at] = slab
        halo_out[side] = slab.astype(bf16)
        copy = pltpu.make_async_remote_copy(
            src_ref=halo_out.at[side],
            dst_ref=halo_in.at[side],
            send_sem=send_h.at[side],
            recv_sem=recv_h.at[side],
            device_id={"rng": halo_partners[side]},
            device_id_type=MESH,
        )
        copy.start()
        halo_copies.append(copy)
    level[64:576] = magnitude(slice(64, 576))

    def sweeps(u):
        for sweep in range(SWEEPS):
            diff = u[1:] - u[:-1]
            flux = diff / (2.0 + 0.5 * (diff * diff))
            u = u[1:-1] + (flux[1:] - flux[:-1])
        return u

    def spread(h, carry):
        at = pl.ds(pl.multiple_of(h * LANES, LANES), LANES)
        out_ref[h] = sweeps(level[:, at].reshape(80, 8, LANES)).reshape(512, LANES)
        return carry

    lax.fori_loop(0, 2, spread, 0)
    for copy in halo_copies:
        copy.wait_recv()

    place = lax.broadcasted_iota(jnp.int32, (8, 8, LANES), 1)

    def backward(v):
        return jnp.concatenate([v[7 - j : 8 - j] for j in range(8)], axis=0)

    def mend(h, carry):
        at = pl.ds(pl.multiple_of(h * LANES, LANES), LANES)
        first = level[64:192, at].reshape(16, 8, LANES)
        last = level[448:576, at].reshape(16, 8, LANES)
        above = halo_in[0, :, at].astype(f32).reshape(8, 8, LANES)
        below = halo_in[1, :, at].astype(f32).reshape(8, 8, LANES)
        below = jnp.where(rng == 0, backward(first[:8]), below)
        above = jnp.where(rng == 7, backward(last[8:]), above)
        u = jnp.concatenate(
            [
                jnp.where(place == 0, below, last[:8]),
                jnp.where(place == 0, first[:8], last[8:]),
                jnp.where(place == 0, first[8:], above),
            ],
            axis=0,
        )
        u = sweeps(u)
        head = out_ref[h, 0:64].reshape(8, 8, LANES)
        out_ref[h, 0:64] = jnp.where(place == 0, u, head).reshape(64, LANES)
        tail = out_ref[h, 448:512].reshape(8, 8, LANES)
        out_ref[h, 448:512] = jnp.where(place == 7, u, tail).reshape(64, LANES)
        return carry

    lax.fori_loop(0, 2, mend, 0)

    for copy in list(a_copies.values()) + list(x_copies.values()) + list(m_copies.values()) + halo_copies:
        copy.wait_send()


def restore(smooth_ref, out_ref):
    for pair in range(4):
        both = [smooth_ref[0, pl.ds(2 * pair + t, 64, stride=8), :] for t in range(2)]
        out_ref[:, pair * LANES : (pair + 1) * LANES] = jnp.concatenate(both, axis=0).T


def per_device(raw_echoes, merge_taps, merge_weights, track_offsets):
    second, twiddle, beam = make_tables()
    vmem = pl.BlockSpec(memory_space=pltpu.VMEM)
    smem = pl.BlockSpec(memory_space=pltpu.SMEM)
    anywhere = pl.BlockSpec(memory_space=pl.ANY)
    dma = pltpu.SemaphoreType.DMA
    smooth = pl.pallas_call(
        kernel,
        out_shape=jax.ShapeDtypeStruct((2, 512, LANES), f32),
        in_specs=[anywhere, anywhere, anywhere, anywhere, anywhere, anywhere, smem],
        out_specs=vmem,
        scratch_shapes=[
            pltpu.VMEM((2, 128, 4096), bf16),
            pltpu.VMEM((4, 256, 256), bf16),
            pltpu.VMEM((2 * ANG, 512), bf16),
            pltpu.VMEM((2, 32, LANES), f32),
            pltpu.VMEM((MERGES, 2, TAPS, 2 * ANG), jnp.int32),
            pltpu.VMEM((MERGES, 2, TAPS, 2 * ANG), f32),
            pltpu.VMEM((GROUPS, 128, 256), bf16),
            pltpu.VMEM((4, 128, 256), f32),
            pltpu.VMEM((4, CHUNKS, 128, 2 * LANES), bf16),
            pltpu.VMEM((CHUNKS, 4, 128, 2 * LANES), bf16),
            pltpu.VMEM((CHUNKS, ANG, LANES), bf16),
            pltpu.VMEM((CHUNKS, ANG, LANES), bf16),
            pltpu.VMEM((CHUNKS, ANG, LANES), f32),
            pltpu.VMEM((MERGES, CHUNKS, ANG, LANES), bf16),
            pltpu.VMEM((MERGES, CHUNKS, ANG, LANES), bf16),
            pltpu.VMEM((MERGES, 2, CHUNKS, 2, ANG, LANES), f32),
            pltpu.VMEM((MERGES, 2, ANG, ANG), bf16),
            pltpu.VMEM((2, 640, 512), bf16),
            pltpu.VMEM((2, ANG, 512), bf16),
            pltpu.VMEM((640, ANG), f32),
            pltpu.VMEM((2, 64, ANG), bf16),
            pltpu.VMEM((2, 64, ANG), bf16),
            dma((7,)),
            dma((len(UNITS),)),
            dma((len(UNITS), 3)),
            dma((len(UNITS), 3)),
            dma((len(UNITS),)),
            dma((len(UNITS),)),
            dma((MERGES, len(UNITS))),
            dma((MERGES, len(UNITS))),
            dma((2,)),
            dma((2,)),
        ],
        compiler_params=pltpu.CompilerParams(
            collective_id=0, has_side_effects=True, vmem_limit_bytes=56 << 20
        ),
        name="backproject",
    )(
        raw_echoes,
        jnp.asarray(second),
        jnp.asarray(beam),
        jnp.asarray(twiddle),
        merge_taps,
        merge_weights,
        track_offsets,
    )
    return pl.pallas_call(
        restore,
        grid=(2,),
        out_shape=jax.ShapeDtypeStruct((ANG, 512), f32),
        in_specs=[pl.BlockSpec((1, 512, LANES), lambda h: (h, 0, 0))],
        out_specs=pl.BlockSpec((LANES, 512), lambda h: (h, 0)),
        name="restore",
    )(smooth)


def solution(mesh):
    in_specs = (P(None, ("sub", "rng"), None), P(), P(), P())
    out_specs = P("sub", "rng")
    return jax.shard_map(
        per_device, mesh=mesh, in_specs=in_specs, out_specs=out_specs, check_vma=False
    )
```

```python
import functools
import math

import jax
import jax.numpy as jnp
import numpy as np
from jax import lax
from jax.experimental import pallas as pl
from jax.experimental.pallas import tpu as pltpu
from jax.sharding import PartitionSpec as P

FACTOR = 64
ANG = 256
TAPS = 8
MERGES = 4
SWEEPS = 8
PERIOD = 8192
LANES = 128
CHUNKS = 8
UNITS = ((0,), (1,), (2,), (3,), (4,), (5,), (6,), (7,))
GROUPS = 8
MESH = pl.DeviceIdType.MESH

bf16 = jnp.bfloat16
f32 = jnp.float32


def make_tables():
    tile = np.arange(LANES)
    b = np.arange(LANES)
    second = np.zeros((4, 2, LANES, 2, LANES))
    real = tile // 64 == 0
    for g in range(4):
        for half in range(2):
            r = 4 * half + (tile // 16 - g) % 4
            d = 16 * r + tile % 16
            angle = 2.0 * np.pi / 128.0 * ((b[:, None] * d[None, :]) % 128)
            cosine, sine = np.cos(angle) / FACTOR, np.sin(angle) / FACTOR
            second[g, 0, :, half] = np.where(real, cosine, -sine)
            second[g, 1, :, half] = np.where(real, sine, cosine)
    second = second.reshape(4, 2 * LANES, 2 * LANES)
    c = np.arange(32)
    angle = 2.0 * np.pi / 4096.0 * (c[:, None] * b[None, :])
    twiddle = np.stack([np.cos(angle), np.sin(angle)])
    a = np.arange(ANG) - ANG // 2
    q = np.arange(1024)
    angle = 2.0 * np.pi / 1024.0 * ((a[:, None] * q[None, :]) % 1024)
    beam = np.stack([np.cos(angle), np.sin(angle)]) / 32.0
    beam = beam.reshape(2, ANG, 4, 2, LANES).transpose(3, 0, 1, 2, 4).reshape(2, 2 * ANG, 512)
    return (
        second.astype(jnp.bfloat16),
        twiddle.astype(np.float32),
        np.ascontiguousarray(beam).astype(jnp.bfloat16),
    )


def transform_eight(z):
    half = math.sqrt(0.5)

    def four(v):
        (ar, ai), (br, bi), (cr, ci), (dr, di) = v
        sr, si, tr, ti = ar + cr, ai + ci, ar - cr, ai - ci
        ur, ui, vr, vi = br + dr, bi + di, br - dr, bi - di
        return [(sr + ur, si + ui), (tr + vi, ti - vr), (sr - ur, si - ui), (tr - vi, ti + vr)]

    even = four(z[0::2])
    odd = four(z[1::2])
    (o0r, o0i), (o1r, o1i), (o2r, o2i), (o3r, o3i) = odd
    turned = [
        (o0r, o0i),
        ((o1r + o1i) * half, (o1i - o1r) * half),
        (o2i, -o2r),
        ((o3i - o3r) * half, (-o3i - o3r) * half),
    ]
    low = [(er + tr, ei + ti) for (er, ei), (tr, ti) in zip(even, turned)]
    high = [(er - tr, ei - ti) for (er, ei), (tr, ti) in zip(even, turned)]
    return low + high


def unit_circle(steps):
    moved = steps + 1024
    quadrant = moved >> 11
    x = ((moved & 2047) - 1024).astype(f32) * (2.0 * math.pi / PERIOD)
    z = x * x
    sine = x * (1.0 + z * (-1.0 / 6.0 + z * (1.0 / 120.0 - z * (1.0 / 5040.0))))
    cosine = 1.0 + z * (-0.5 + z * (1.0 / 24.0 + z * (-1.0 / 720.0 + z * (1.0 / 40320.0))))
    swap = (quadrant & 1) == 1
    out_cos = jnp.where(swap, sine, cosine)
    out_sin = jnp.where(swap, cosine, sine)
    out_cos = jnp.where(((quadrant + 1) & 2) == 2, -out_cos, out_cos)
    out_sin = jnp.where((quadrant & 2) == 2, -out_sin, out_sin)
    return out_cos, out_sin


def order_of_steps():
    return [
        ("dft", 0), ("dft", 1), ("dft", 2), ("beam", 0), ("dft", 3), ("tab", 0), ("beam", 1),
        ("lead", 0), ("tab", 2), ("beam", 2), ("m0", 0), ("tab", 1), ("lead", 1), ("beam", 3),
        ("m0", 1), ("lead", 2), ("beam", 4), ("m1", 0), ("lead", 3), ("m0", 2), ("beam", 5),
        ("m1", 1), ("m0", 3), ("m2", 0), ("lead", 4), ("beam", 6), ("m1", 2), ("m0", 4),
        ("m2", 1), ("lead", 5), ("beam", 7), ("m1", 3), ("m0", 5), ("m2", 2), ("lead", 6),
        ("tab", 3), ("m1", 4), ("m0", 6), ("m2", 3), ("lead", 7), ("m1", 5), ("m0", 7),
        ("m2", 4), ("m1", 6), ("m3", 1), ("m2", 5), ("perm", 0), ("m1", 7), ("m3", 0),
        ("m2", 6), ("m2", 7), ("m3", 5), ("m3", 2), ("m3", 3), ("m3", 6), ("m3", 4),
        ("m3", 7),
    ]


def kernel(
    raw_hbm, second_hbm, beam_hbm, twiddle_hbm, taps_hbm, weights_hbm, offsets_ref, out_ref,
    raw, second, beam, twiddle_ref, taps_ref, weights_ref, rows_buf, wide, sent, got, part_out, part_in, part_own,
    image, image_in, phase, mats, perm, final, level, halo_out, halo_in,
    in_sem, own_sem, send_a, recv_a, send_x, recv_x, send_m, recv_m, send_h, recv_h,
):
    sub = lax.axis_index("sub")
    rng = lax.axis_index("rng")
    x_lo = rng % 2
    y = rng // 2

    half_bits = [(sub // 2**l) % 2 for l in range(MERGES)]
    partners = [sub + 2**l - 2 * 2**l * half_bits[l] for l in range(MERGES)]
    x_partner = rng + 1 - 2 * x_lo
    y_partners = [((y + j) % 4) * 2 + x_lo for j in (1, 2, 3)]
    halo_partners = [(rng + 7) % 8, (rng + 1) % 8]

    raw_copies = [
        pltpu.make_async_copy(raw_hbm.at[:, pl.ds(64 * h, 64)], raw.at[:, pl.ds(64 * h, 64)], in_sem.at[h])
        for h in range(2)
    ]
    second_copy = pltpu.make_async_copy(second_hbm, second, in_sem.at[2])
    beam_copy = pltpu.make_async_copy(beam_hbm.at[x_lo], beam, in_sem.at[3])
    twiddle_copy = pltpu.make_async_copy(twiddle_hbm, twiddle_ref, in_sem.at[4])
    taps_copy = pltpu.make_async_copy(taps_hbm, taps_ref, in_sem.at[5])
    weights_copy = pltpu.make_async_copy(weights_hbm, weights_ref, in_sem.at[6])
    twiddle_copy.start()
    for copy in raw_copies:
        copy.start()
    second_copy.start()
    beam_copy.start()
    taps_copy.start()
    weights_copy.start()

    barrier = pltpu.get_barrier_semaphore()
    ids = [{"rng": t} for t in y_partners + [x_partner] + halo_partners] + [{"sub": t} for t in partners]
    for one in ids:
        pl.semaphore_signal(barrier, inc=1, device_id=one, device_id_type=MESH)

    lane = lax.broadcasted_iota(jnp.int32, (16, LANES), 1)
    group_bits = [((lane // 16) // 2**t) % 2 == 1 for t in range(2)]
    a_copies = {}
    own_copies = {}

    def transform(i, first):
        def rows(block, carry):
            at = pl.ds(pl.multiple_of(block * 16, 16), 16)

            def load(part, a):
                return raw[part, at, a * LANES : (a + 1) * LANES].astype(f32)

            mixed = []
            for m in range(8):
                v = [(load(0, m + 8 * j), load(1, m + 8 * j)) for j in range(4)]
                if i % 2 == 0:
                    sr, si = v[0][0] + v[2][0], v[0][1] + v[2][1]
                    tr, ti = v[1][0] + v[3][0], v[1][1] + v[3][1]
                    zr, zi = (sr + tr, si + ti) if i == 0 else (sr - tr, si - ti)
                else:
                    sr, si = v[0][0] - v[2][0], v[0][1] - v[2][1]
                    tr, ti = v[1][0] - v[3][0], v[1][1] - v[3][1]
                    zr, zi = (sr + ti, si - tr) if i == 1 else (sr - ti, si + tr)
                if i * m:
                    turn = 2.0 * math.pi * i * m / 32.0
                    wc, ws = math.cos(turn), math.sin(turn)
                    zr, zi = zr * wc + zi * ws, zi * wc - zr * ws
                mixed.append((zr, zi))
            for g, (zr, zi) in enumerate(transform_eight(mixed)):
                c = i + 4 * g
                wc = twiddle_ref[0, c : c + 1, :]
                ws = twiddle_ref[1, c : c + 1, :]
                rows_buf[g, at, 0:LANES] = (zr * wc + zi * ws).astype(bf16)
                rows_buf[g, at, LANES : 2 * LANES] = (zi * wc - zr * ws).astype(bf16)
            return carry

        if first:
            twiddle_copy.wait()
            raw_copies[0].wait()
            lax.fori_loop(0, 4, rows, 0, unroll=2)
            raw_copies[1].wait()
            lax.fori_loop(4, 8, rows, 0, unroll=2)
            second_copy.wait()
        else:
            lax.fori_loop(0, 8, rows, 0, unroll=2)
        for odd in range(2):
            for g in range(4):
                wide[g] = jnp.dot(rows_buf[2 * g + odd], second[g], preferred_element_type=f32)
            share(2 * i + odd, first and odd == 0)

    def share(i, first):
        def pick(block, carry):
            at = pl.ds(pl.multiple_of(block * 16, 16), 16)
            for part in range(2):
                tiles = [wide[(4 - r) % 4, at, part * LANES : (part + 1) * LANES] for r in range(4)]
                for t in range(2):
                    tiles = [jnp.where(group_bits[t], tiles[(r - 2**t) % 4], tiles[r]) for r in range(4)]
                for r in range(4):
                    sent[2 * part + r // 2, i, at, (r % 2) * LANES : (r % 2 + 1) * LANES] = tiles[r].astype(bf16)
            return carry

        lax.fori_loop(0, 8, pick, 0, unroll=4)
        if first:
            pl.semaphore_wait(barrier, len(ids))
        for n, unit in enumerate(UNITS):
            if unit[-1] == i:
                send_unit(n, pl.ds(unit[0], len(unit)))

    def send_unit(n, at):
        for j in (2, 1, 3):
            target = (y + j) % 4
            copy = pltpu.make_async_remote_copy(
                src_ref=sent.at[target, at],
                dst_ref=got.at[at, y],
                send_sem=send_a.at[n, j - 1],
                recv_sem=recv_a.at[n, j - 1],
                device_id={"rng": target * 2 + x_lo},
                device_id_type=MESH,
            )
            copy.start()
            a_copies[n, j] = copy
        own_copies[n] = pltpu.make_async_copy(sent.at[y, at], got.at[at, y], own_sem.at[n])
        own_copies[n].start()

    angle_rows = lax.broadcasted_iota(jnp.int32, (ANG, ANG), 0)
    sectors = [sub * 0]
    for l in range(MERGES - 1):
        sectors.append(sectors[l] * 2 + half_bits[l])

    def tables(l):
        if l == 0:
            taps_copy.wait()
            weights_copy.wait()
        bit = half_bits[l]
        for which in range(2):
            half = bit if which == 0 else 1 - bit
            at = pl.ds(pl.multiple_of(bit * ANG, ANG), ANG)
            taps = taps_ref[l, half, :, at]
            weights = weights_ref[l, half, :, at]
            total = jnp.zeros((ANG, ANG), f32)
            for t in range(TAPS):
                total = total + jnp.where(taps[t : t + 1, :] == angle_rows, weights[t : t + 1, :], 0.0)
            mats[l, which] = total.T.astype(bf16)
            offset = offsets_ref[l, sub] if which == 0 else offsets_ref[l, partners[l]]
            anchor = sectors[l] * (2 * ANG) + bit * ANG

            def fill(block, carry, which=which, offset=offset, anchor=anchor):
                start = pl.multiple_of(block * 32, 32)
                at = pl.ds(start, 32)
                row = lax.broadcasted_iota(jnp.int32, (32, LANES), 0)
                col = lax.broadcasted_iota(jnp.int32, (32, LANES), 1)
                column = 512 * rng + 32 * (col & 15) + 8 * (((col >> 4) - rng) & 3) + 1
                slope = (offset * (anchor + start + row)) & (PERIOD - 1)
                er, ei = unit_circle((slope * column) & (PERIOD - 1))
                tr, ti = unit_circle(slope)
                er, ei = er * 0.7071067811865476, ei * 0.7071067811865476
                ei = jnp.where(col < 64, -ei, ei)
                ti = jnp.where(col < 64, -ti, ti)
                for i in range(CHUNKS):
                    phase[l, which, 2 * (i % 4) + i // 4, 0, at] = er
                    phase[l, which, 2 * (i % 4) + i // 4, 1, at] = ei
                    if i < CHUNKS - 1:
                        er, ei = er * tr - ei * ti, er * ti + ei * tr
                return carry

            lax.fori_loop(0, ANG // 32, fill, 0, unroll=2)

    def orders():
        for i in range(4):
            row = lax.broadcasted_iota(jnp.int32, (640, LANES), 0)
            col = lax.broadcasted_iota(jnp.int32, (640, LANES), 1)
            wanted = (64 * (row & 7) + (row >> 3) - 8) & 511
            place = 32 * (col & 15) + 8 * (((col >> 4) - rng) & 3) + i
            late = 4 * (col >> 6)
            for part in range(2):
                here = place + (late if part == 0 else 4 - late) == wanted
                perm[part, :, i * LANES : (i + 1) * LANES] = jnp.where(here, 1.0, 0.0).astype(bf16)

    x_copies = {}
    m_copies = {}

    def contribution(l, which, unit, ref):
        proj = jnp.dot(
            mats[l, which],
            jnp.concatenate([ref[l, q] for q in unit], axis=1),
            preferred_element_type=f32,
        )
        parts = [proj[:, t * LANES : (t + 1) * LANES] for t in range(len(unit))]
        return [
            part * phase[l, which, q, 0] + pltpu.roll(part, 64, 1) * phase[l, which, q, 1]
            for part, q in zip(parts, unit)
        ]

    def pass_on(l, n):
        at = pl.ds(UNITS[n][0], len(UNITS[n]))
        copy = pltpu.make_async_remote_copy(
            src_ref=image.at[l, at],
            dst_ref=image_in.at[l, at],
            send_sem=send_m.at[l, n],
            recv_sem=recv_m.at[l, n],
            device_id={"sub": partners[l]},
            device_id_type=MESH,
        )
        copy.start()
        m_copies[l, n] = copy

    def step(kind, n):
        if kind == "dft":
            transform(n, n == 0)
            return
        if kind == "tab":
            tables(n)
            return
        if kind == "perm":
            orders()
            return
        unit = UNITS[n]
        if kind == "beam":
            if n == 0:
                beam_copy.wait()
            for j in (1, 2, 3):
                a_copies[n, j].wait_recv()
            own_copies[n].wait()
            both = jnp.concatenate([got[q].reshape(512, 2 * LANES) for q in unit], axis=1)
            total = jnp.dot(beam[...], both, preferred_element_type=f32)
            is_low = x_lo == 0
            owned = []
            for t, q in enumerate(unit):
                low, high = [
                    total[:ANG, at] + turned * pltpu.roll(total[ANG:, at], 64, 1)
                    for at in (slice(2 * t * LANES, (2 * t + 1) * LANES), slice((2 * t + 1) * LANES, (2 * t + 2) * LANES))
                ]
                part_out[q] = jnp.where(is_low, high, low).astype(bf16)
                owned.append(jnp.where(is_low, low, high))
            at = pl.ds(unit[0], len(unit))
            copy = pltpu.make_async_remote_copy(
                src_ref=part_out.at[at],
                dst_ref=part_in.at[at],
                send_sem=send_x.at[n],
                recv_sem=recv_x.at[n],
                device_id={"rng": x_partner},
                device_id_type=MESH,
            )
            copy.start()
            x_copies[n] = copy
            for q, value in zip(unit, owned):
                part_own[q] = value
        elif kind == "lead":
            x_copies[n].wait_recv()
            for q in unit:
                image[0, q] = (part_own[q] + part_in[q].astype(f32)).astype(bf16)
            pass_on(0, n)
        else:
            l = int(kind[1])
            m_copies[l, n].wait_recv()
            mine = contribution(l, 0, unit, image)
            theirs = contribution(l, 1, unit, image_in)
            for q, a, b in zip(unit, mine, theirs):
                merged = a + b
                if l < MERGES - 1:
                    image[l + 1, q] = merged.astype(bf16)
                    continue
                tile = (q // 2) * LANES
                if q % 2 == 0:
                    final[0, :, tile : tile + 64] = merged[:, :64].astype(bf16)
                    final[1, :, tile + 64 : tile + LANES] = merged[:, 64:].astype(bf16)
                else:
                    turn = pltpu.roll(merged, 64, 1)
                    final[1, :, tile : tile + 64] = turn[:, :64].astype(bf16)
                    final[0, :, tile + 64 : tile + LANES] = turn[:, 64:].astype(bf16)
            if l < MERGES - 1:
                pass_on(l + 1, n)

    turned = jnp.where(lax.broadcasted_iota(jnp.int32, (ANG, LANES), 1) < 64, 1.0, -1.0)
    for kind, i in order_of_steps():
        step(kind, i)

    def magnitude(at):
        re = lax.dot_general(perm[0, at], final[0], (((1,), (1,)), ((), ())), preferred_element_type=f32)
        im = lax.dot_general(perm[1, at], final[1], (((1,), (1,)), ((), ())), preferred_element_type=f32)
        return jnp.sqrt(re * re + im * im)

    halo_copies = []
    for side in range(2):
        at = slice(0, 64) if side else slice(576, 640)
        slab = magnitude(at)
        level[at] = slab
        halo_out[side] = slab.astype(bf16)
        copy = pltpu.make_async_remote_copy(
            src_ref=halo_out.at[side],
            dst_ref=halo_in.at[side],
            send_sem=send_h.at[side],
            recv_sem=recv_h.at[side],
            device_id={"rng": halo_partners[side]},
            device_id_type=MESH,
        )
        copy.start()
        halo_copies.append(copy)
    level[64:576] = magnitude(slice(64, 576))

    def sweeps(u):
        for sweep in range(SWEEPS):
            diff = u[1:] - u[:-1]
            flux = diff / (2.0 + 0.5 * (diff * diff))
            u = u[1:-1] + (flux[1:] - flux[:-1])
        return u

    def spread(h, carry):
        at = pl.ds(pl.multiple_of(h * LANES, LANES), LANES)
        out_ref[h] = sweeps(level[:, at].reshape(80, 8, LANES)).reshape(512, LANES)
        return carry

    lax.fori_loop(0, 2, spread, 0, unroll=True)
    for copy in halo_copies:
        copy.wait_recv()

    place = lax.broadcasted_iota(jnp.int32, (8, 8, LANES), 1)

    def backward(v):
        return jnp.concatenate([v[7 - j : 8 - j] for j in range(8)], axis=0)

    def mend(h, carry):
        at = pl.ds(pl.multiple_of(h * LANES, LANES), LANES)
        first = level[64:192, at].reshape(16, 8, LANES)
        last = level[448:576, at].reshape(16, 8, LANES)
        above = halo_in[0, :, at].astype(f32).reshape(8, 8, LANES)
        below = halo_in[1, :, at].astype(f32).reshape(8, 8, LANES)
        below = jnp.where(rng == 0, backward(first[:8]), below)
        above = jnp.where(rng == 7, backward(last[8:]), above)
        u = jnp.concatenate(
            [
                jnp.where(place == 0, below, last[:8]),
                jnp.where(place == 0, first[:8], last[8:]),
                jnp.where(place == 0, first[8:], above),
            ],
            axis=0,
        )
        u = sweeps(u)
        head = out_ref[h, 0:64].reshape(8, 8, LANES)
        out_ref[h, 0:64] = jnp.where(place == 0, u, head).reshape(64, LANES)
        tail = out_ref[h, 448:512].reshape(8, 8, LANES)
        out_ref[h, 448:512] = jnp.where(place == 7, u, tail).reshape(64, LANES)
        return carry

    lax.fori_loop(0, 2, mend, 0, unroll=True)

    for copy in list(a_copies.values()) + list(x_copies.values()) + list(m_copies.values()) + halo_copies:
        copy.wait_send()


def restore(smooth_ref, out_ref):
    for pair in range(4):
        both = [smooth_ref[0, pl.ds(2 * pair + t, 64, stride=8), :] for t in range(2)]
        out_ref[:, pair * LANES : (pair + 1) * LANES] = jnp.concatenate(both, axis=0).T


def per_device(raw_echoes, merge_taps, merge_weights, track_offsets):
    second, twiddle, beam = make_tables()
    vmem = pl.BlockSpec(memory_space=pltpu.VMEM)
    smem = pl.BlockSpec(memory_space=pltpu.SMEM)
    anywhere = pl.BlockSpec(memory_space=pl.ANY)
    dma = pltpu.SemaphoreType.DMA
    smooth = pl.pallas_call(
        kernel,
        out_shape=jax.ShapeDtypeStruct((2, 512, LANES), f32),
        in_specs=[anywhere, anywhere, anywhere, anywhere, anywhere, anywhere, smem],
        out_specs=vmem,
        scratch_shapes=[
            pltpu.VMEM((2, 128, 4096), bf16),
            pltpu.VMEM((4, 256, 256), bf16),
            pltpu.VMEM((2 * ANG, 512), bf16),
            pltpu.VMEM((2, 32, LANES), f32),
            pltpu.VMEM((MERGES, 2, TAPS, 2 * ANG), jnp.int32),
            pltpu.VMEM((MERGES, 2, TAPS, 2 * ANG), f32),
            pltpu.VMEM((GROUPS, 128, 256), bf16),
            pltpu.VMEM((4, 128, 256), f32),
            pltpu.VMEM((4, CHUNKS, 128, 2 * LANES), bf16),
            pltpu.VMEM((CHUNKS, 4, 128, 2 * LANES), bf16),
            pltpu.VMEM((CHUNKS, ANG, LANES), bf16),
            pltpu.VMEM((CHUNKS, ANG, LANES), bf16),
            pltpu.VMEM((CHUNKS, ANG, LANES), f32),
            pltpu.VMEM((MERGES, CHUNKS, ANG, LANES), bf16),
            pltpu.VMEM((MERGES, CHUNKS, ANG, LANES), bf16),
            pltpu.VMEM((MERGES, 2, CHUNKS, 2, ANG, LANES), f32),
            pltpu.VMEM((MERGES, 2, ANG, ANG), bf16),
            pltpu.VMEM((2, 640, 512), bf16),
            pltpu.VMEM((2, ANG, 512), bf16),
            pltpu.VMEM((640, ANG), f32),
            pltpu.VMEM((2, 64, ANG), bf16),
            pltpu.VMEM((2, 64, ANG), bf16),
            dma((7,)),
            dma((len(UNITS),)),
            dma((len(UNITS), 3)),
            dma((len(UNITS), 3)),
            dma((len(UNITS),)),
            dma((len(UNITS),)),
            dma((MERGES, len(UNITS))),
            dma((MERGES, len(UNITS))),
            dma((2,)),
            dma((2,)),
        ],
        compiler_params=pltpu.CompilerParams(
            collective_id=0, has_side_effects=True, vmem_limit_bytes=56 << 20
        ),
        name="backproject",
    )(
        raw_echoes,
        jnp.asarray(second),
        jnp.asarray(beam),
        jnp.asarray(twiddle),
        merge_taps,
        merge_weights,
        track_offsets,
    )
    return pl.pallas_call(
        restore,
        grid=(2,),
        out_shape=jax.ShapeDtypeStruct((ANG, 512), f32),
        in_specs=[pl.BlockSpec((1, 512, LANES), lambda h: (h, 0, 0))],
        out_specs=pl.BlockSpec((LANES, 512), lambda h: (h, 0)),
        name="restore",
    )(smooth)


def solution(mesh):
    in_specs = (P(None, ("sub", "rng"), None), P(), P(), P())
    out_specs = P("sub", "rng")
    return jax.shard_map(
        per_device, mesh=mesh, in_specs=in_specs, out_specs=out_specs, check_vma=False
    )
```
